256 devices in a mesh: row: 16 (over y, x), col: 2 (over core), ctx: 8 (over z).
Axes of the slice: x: 4, y: 4, z: 8, core: 2. Of those that a mesh axis runs over, the one named last changes fastest.
Arguments:
- queries: bfloat16 [8192, 6144], P(('col', 'ctx'), 'row'), may hold values from -16 to 16
- keys: bfloat16 [8192, 6144], P(('col', 'ctx'), 'row'), may hold values from -16 to 16
- values: bfloat16 [8192, 6144], P(('col', 'ctx'), 'row'), may hold values from -6 to 6
- out_weight: bfloat16 [6144, 6144], P('col', 'row'), may hold values from -0.078125 to 0.078125
- cotangent: bfloat16 [8192, 6144], P(('col', 'ctx'), 'row'), may hold values from -0.125 to 0.125
- block_mask: int32 [16, 16], replicated, may hold values from 0 to 1, as said below
Outputs:
- mixed_out: bfloat16 [8192, 6144], P(('col', 'ctx'), 'row')
- grad_weight: bfloat16 [6144, 6144], P(('col', 'ctx'), 'row')
The draws below stay inside these ranges and needn't reach their ends.
Inputs may be any that keep to these rules, and one draw needn't show every extreme that they name: block_mask[i, i] is 1 for every block i, and block_mask[i, j] is 0 for j > i.
All inputs are finite; a program needn't handle non-finite values.
Results may differ from the reference program's by a relative error of at most 0.013.
Values may be sent and summed in bfloat16 or wider, within the bound.
A program may use at most 64 MiB of HBM per device.

```python
import math
import jax
import jax.numpy as jnp
from jax import lax

D = 6144
H = 48
HD = 128
BLOCK = 512
SEQ = 8192
NBLK = 16


def drawn_pair(key):
    base_key = jax.random.fold_in(key, 7)
    query_key, keys_key = jax.random.split(base_key, 2)
    query_draw = jnp.clip(jax.random.normal(query_key, (SEQ, D), jnp.float32), -6.0, 6.0) * 1.6
    key_draw = jnp.clip(jax.random.normal(keys_key, (SEQ, D), jnp.float32), -6.0, 6.0) * 1.6
    return (query_draw, key_draw)


def draw_queries(key, part):
    return drawn_pair(key)[0].astype(jnp.bfloat16)


def draw_keys(key, part):
    return drawn_pair(key)[1].astype(jnp.bfloat16)


def draw_block_mask(key, part):
    random_bits = jax.random.randint(jax.random.fold_in(key, 11), (NBLK, NBLK), 0, 2, dtype=jnp.int32)
    row_index = jnp.arange(NBLK, dtype=jnp.int32)[:, None]
    column_index = jnp.arange(NBLK, dtype=jnp.int32)[None, :]
    ones_block = jnp.ones((NBLK, NBLK), jnp.int32)
    zero_block = jnp.zeros((NBLK, NBLK), jnp.int32)
    return jnp.where(column_index == row_index, ones_block, jnp.where(column_index < row_index, random_bits, zero_block)).astype(jnp.int32)


def block_scale(key, dims, pieces, low, high):
    gain = 1.0
    for axis_at, blocks in pieces:
        draws = jax.random.uniform(jax.random.fold_in(jax.random.fold_in(key, 6), axis_at), (blocks,), jnp.float32, low / len(pieces), high / len(pieces))
        gain = gain * jnp.repeat(jnp.exp(draws), dims[axis_at] // blocks).reshape((-1,) + (1,) * (len(dims) - 1 - axis_at))
    return gain


def scatter_about(key, shape, width, bound, cuts=(), kind=jnp.bfloat16):
    result = jax.random.normal(key, shape, jnp.float32) * width
    if len(cuts) > 0:
        result = block_scale(key, shape, cuts, -0.22, 0.18) * result
    return jnp.clip(result, min=-bound, max=bound).astype(kind)


def setup_inputs(seed: int = 0) -> dict:
    seeds = jax.random.split(jax.random.key(seed), 7)
    return {
        "queries": draw_queries(jax.random.fold_in(seeds[6], 71), 0),
        "keys": draw_keys(jax.random.fold_in(seeds[6], 71), 0),
        "values": scatter_about(seeds[2], (SEQ, D), 1.0, 6.0, ((0, 16), (1, 16))),
        "out_weight": scatter_about(seeds[3], (D, D), D ** -0.5, 0.078125, ((0, 2), (1, 16))),
        "cotangent": scatter_about(seeds[4], (SEQ, D), 0.02, 0.125, ((0, 16), (1, 16))),
        "block_mask": draw_block_mask(jax.random.fold_in(seeds[6], 71), 0),
    }


NEGATIVE_FILL = -1e+30

def attend_head(query_head, key_head, value_head, block_mask):
    score_scale = 1.0 / math.sqrt(HD)

    def query_block(block_index):
        query_rows = lax.dynamic_slice_in_dim(query_head, block_index * BLOCK, BLOCK, 0)
        scores = jnp.dot(query_rows, key_head.T, preferred_element_type=jnp.float32) * score_scale
        mask_row = lax.dynamic_index_in_dim(block_mask, block_index, 0, keepdims=False)
        allowed = jnp.repeat(mask_row, BLOCK, total_repeat_length=SEQ) == 1
        scores = jnp.where(allowed[None, :], scores, NEGATIVE_FILL)
        row_max = lax.optimization_barrier(jnp.max(scores, axis=1, keepdims=True))
        weights = jnp.where(allowed[None, :], jnp.exp(scores - row_max), 0.0)
        row_sum = lax.optimization_barrier(jnp.sum(weights, axis=1, keepdims=True))
        weighted = jnp.dot(weights.astype(jnp.bfloat16), value_head, preferred_element_type=jnp.float32)
        return (weighted / row_sum).astype(jnp.bfloat16)
    blocks_out = lax.map(query_block, jnp.arange(NBLK, dtype=jnp.int32))
    return blocks_out.reshape(SEQ, HD)

def reference(queries, keys, values, out_weight, cotangent, block_mask):

    def per_head(head_index):
        offset = head_index * HD
        query_head = lax.dynamic_slice_in_dim(queries, offset, HD, 1)
        key_head = lax.dynamic_slice_in_dim(keys, offset, HD, 1)
        value_head = lax.dynamic_slice_in_dim(values, offset, HD, 1)
        return attend_head(query_head, key_head, value_head, block_mask)
    heads_out = lax.map(per_head, jnp.arange(H, dtype=jnp.int32))
    attended = jnp.transpose(heads_out, (1, 0, 2)).reshape(SEQ, D)
    mixed_out = jnp.dot(attended, out_weight, preferred_element_type=jnp.float32).astype(jnp.bfloat16)
    grad_weight = jnp.dot(attended.T, cotangent, preferred_element_type=jnp.float32).astype(jnp.bfloat16)
    return (mixed_out, grad_weight)
```

```python
import functools
import math

import jax
import jax.numpy as jnp
from jax import lax
from jax.experimental import pallas as pl
from jax.experimental.pallas import tpu as pltpu
from jax.sharding import PartitionSpec as P

HD = 128
BLOCK = 512


def attend_kernel(place_ref, mask_ref, q_ref, k_ref, v_ref, out_ref, run_max, run_sum, weighted):
    back = pl.program_id(1)
    block = place_ref[0] - back
    rate = math.log2(math.e) / math.sqrt(HD)

    @pl.when(back == 0)
    def _():
        run_max[...] = jnp.full_like(run_max, -1e30)
        run_sum[...] = jnp.zeros_like(run_sum)
        weighted[...] = jnp.zeros_like(weighted)

    @pl.when((block >= 0) & (mask_ref[jnp.maximum(block, 0)] == 1))
    def _():
        scores = lax.dot_general(
            q_ref[...], k_ref[...], (((1,), (1,)), ((), ())), preferred_element_type=jnp.float32
        )
        new_max = jnp.maximum(run_max[...], jnp.max(scores, axis=1, keepdims=True))
        correction = jnp.exp2((run_max[...] - new_max) * rate)
        weights = jnp.exp2((scores - new_max) * rate)
        run_sum[...] = run_sum[...] * correction + jnp.sum(weights, axis=1, keepdims=True)
        weighted[...] = weighted[...] * correction + jnp.dot(
            weights.astype(jnp.bfloat16), v_ref[...], preferred_element_type=jnp.float32
        )
        run_max[...] = new_max

    @pl.when(back == pl.num_programs(1) - 1)
    def _():
        out_ref[...] = (weighted[...] / run_sum[...]).astype(out_ref.dtype)


def attend(place, mask_row, queries, keys, values):
    rows, width = queries.shape
    blocks = keys.shape[0] // BLOCK
    heads = width // HD
    kv_spec = pl.BlockSpec((BLOCK, HD), lambda h, b, place, mask: (jnp.maximum(place[0] - b, 0), h))
    q_spec = pl.BlockSpec((BLOCK, HD), lambda h, b, place, mask: (0, h))
    return pl.pallas_call(
        attend_kernel,
        out_shape=jax.ShapeDtypeStruct((rows, width), jnp.bfloat16),
        grid_spec=pltpu.PrefetchScalarGridSpec(
            num_scalar_prefetch=2,
            grid=(heads, blocks),
            in_specs=[q_spec, kv_spec, kv_spec],
            out_specs=q_spec,
            scratch_shapes=[
                pltpu.VMEM((rows, 1), jnp.float32),
                pltpu.VMEM((rows, 1), jnp.float32),
                pltpu.VMEM((rows, HD), jnp.float32),
            ],
        ),
        compiler_params=pltpu.CompilerParams(
            dimension_semantics=("arbitrary", "arbitrary"), vmem_limit_bytes=32 << 20
        ),
    )(place, mask_row, queries, keys, values)


def body(queries, keys, values, out_weight, cotangent, block_mask):
    place = lax.axis_index(("col", "ctx"))
    mask_row = lax.dynamic_index_in_dim(block_mask, place, 0, keepdims=False)
    all_keys = lax.all_gather(keys, ("col", "ctx"), axis=0, tiled=True)
    all_values = lax.all_gather(values, ("col", "ctx"), axis=0, tiled=True)
    weight = lax.all_gather(out_weight, "col", axis=0, tiled=True)
    attended = attend(place.reshape(1), mask_row, queries, all_keys, all_values)
    all_heads = lax.all_gather(attended, "row", axis=1, tiled=True)
    partial = lax.dot_general(
        all_heads, cotangent, (((0,), (0,)), ((), ())), preferred_element_type=jnp.float32
    ).astype(jnp.bfloat16)
    grad_weight = lax.psum_scatter(partial, ("col", "ctx"), scatter_dimension=0, tiled=True)
    mixed_out = jnp.dot(all_heads, weight, preferred_element_type=jnp.float32)
    return (mixed_out.astype(jnp.bfloat16), grad_weight)


def solution(mesh):
    tokens = P(("col", "ctx"), "row")
    return jax.shard_map(
        body,
        mesh=mesh,
        in_specs=(tokens, tokens, tokens, P("col", "row"), tokens, P()),
        out_specs=(tokens, tokens),
        check_vma=False,
    )
```

```python
import functools
import math

import jax
import jax.numpy as jnp
from jax import lax
from jax.experimental import pallas as pl
from jax.experimental.pallas import tpu as pltpu
from jax.sharding import PartitionSpec as P

HD = 128
BLOCK = 512
SIDE = 4
ROWS = SIDE * SIDE
DEPTH = 8
HALF = HD // 2
QUARTER = HD // 4
MESH = pl.DeviceIdType.MESH


def attend_kernel(place_ref, mask_ref, q_ref, k_ref, v_ref, out_ref, run_max, run_sum, weighted):
    back = pl.program_id(1)
    block = place_ref[0] - back
    rate = math.log2(math.e) / math.sqrt(HD)

    @pl.when(back == 0)
    def _():
        run_max[...] = jnp.full_like(run_max, -1e30)
        run_sum[...] = jnp.zeros_like(run_sum)
        weighted[...] = jnp.zeros_like(weighted)

    @pl.when((block >= 0) & (mask_ref[jnp.maximum(block, 0)] == 1))
    def _():
        scores = lax.dot_general(
            q_ref[...], k_ref[...], (((1,), (1,)), ((), ())), preferred_element_type=jnp.float32
        )
        new_max = jnp.maximum(run_max[...], jnp.max(scores, axis=1, keepdims=True))
        correction = jnp.exp2((run_max[...] - new_max) * rate)
        weights = jnp.exp2((scores - new_max) * rate)
        run_sum[...] = run_sum[...] * correction + jnp.sum(weights, axis=1, keepdims=True)
        weighted[...] = weighted[...] * correction + jnp.dot(
            weights.astype(jnp.bfloat16), v_ref[...], preferred_element_type=jnp.float32
        )
        run_max[...] = new_max

    @pl.when(back == pl.num_programs(1) - 1)
    def _():
        out_ref[0] = (weighted[...] / run_sum[...]).T.astype(out_ref.dtype)


def attend(place, mask_row, queries, keys, values):
    rows, width = queries.shape
    blocks = keys.shape[0] // BLOCK
    heads = width // HD
    kv_spec = pl.BlockSpec((BLOCK, HD), lambda h, b, place, mask: (jnp.maximum(place[0] - b, 0), h))
    q_spec = pl.BlockSpec((BLOCK, HD), lambda h, b, place, mask: (0, h))
    return pl.pallas_call(
        attend_kernel,
        out_shape=jax.ShapeDtypeStruct((heads, HD, rows), jnp.bfloat16),
        grid_spec=pltpu.PrefetchScalarGridSpec(
            num_scalar_prefetch=2,
            grid=(heads, blocks),
            in_specs=[q_spec, kv_spec, kv_spec],
            out_specs=pl.BlockSpec((1, HD, BLOCK), lambda h, b, place, mask: (h, 0, 0)),
            scratch_shapes=[
                pltpu.VMEM((rows, 1), jnp.float32),
                pltpu.VMEM((rows, 1), jnp.float32),
                pltpu.VMEM((rows, HD), jnp.float32),
            ],
        ),
        compiler_params=pltpu.CompilerParams(
            dimension_semantics=("arbitrary", "arbitrary"), vmem_limit_bytes=32 << 20
        ),
    )(place, mask_row, queries, keys, values)


def project_kernel(
    att_ref, w_ref, cot_ref, mixed_ref, grad_ref,
    gath, weight, mixed_sum, kept, pair_out, pair_in, ring_out, ring_in,
    ag_send, ag_recv, w_send, w_recv, w_local, pair_send, pair_recv, ring_send, ring_recv,
):
    me = lax.axis_index("row")
    core = lax.axis_index("col")
    z = lax.axis_index("ctx")
    here = (lax.rem(me, SIDE), lax.div(me, SIDE))
    heads = att_ref.shape[0]

    def shifted(value, by, size):
        return lax.rem(value + (by + size), size)

    def block_at(half, first, second):
        by = (first, second) if half == 0 else (second, first)
        return shifted(here[1], by[1], SIDE) * SIDE + shifted(here[0], by[0], SIDE)

    def up(by):
        return {"ctx": shifted(z, by, DEPTH)}

    sibling = {"col": 1 - core}

    barrier = pltpu.get_barrier_semaphore()
    for first, second in ((1, 0), (-1, 0), (0, 1), (0, -1)):
        pl.semaphore_signal(barrier, inc=1, device_id={"row": block_at(0, first, second)}, device_id_type=MESH)
    for by in (1, -1):
        pl.semaphore_signal(barrier, inc=1, device_id=up(by), device_id_type=MESH)
    pl.semaphore_signal(barrier, inc=1, device_id=sibling, device_id_type=MESH)
    pl.semaphore_wait(barrier, 7)

    def put(e, half, block, quarter, leg, by, slot):
        low = half * HALF + (0 if quarter is None else quarter * QUARTER)
        ref = gath.at[e, block, pl.ds(low, HALF if quarter is None else QUARTER)]
        to = block_at(half, by, 0) if leg == 0 else block_at(half, 0, by)
        return pltpu.make_async_remote_copy(
            src_ref=ref, dst_ref=ref, send_sem=ag_send.at[e, half, slot], recv_sem=ag_recv.at[e, half, block],
            device_id={"row": to}, device_id_type=MESH,
        )

    def arrived(e, half, block):
        put(e, half, block, None, 0, 1, 0).wait_recv()

    def send_weight():
        return pltpu.make_async_remote_copy(
            src_ref=w_ref, dst_ref=weight.at[core], send_sem=w_send, recv_sem=w_recv,
            device_id=sibling, device_id_type=MESH,
        )

    def send_pair(e):
        return pltpu.make_async_remote_copy(
            src_ref=pair_out.at[e], dst_ref=pair_in.at[e], send_sem=pair_send.at[e], recv_sem=pair_recv.at[e],
            device_id=sibling, device_id_type=MESH,
        )

    def send_ring(e, way, step):
        rows = pl.ds(way * HALF, HALF) if step == 0 else pl.ds(0, HD)
        return pltpu.make_async_remote_copy(
            src_ref=ring_out.at[e, way, step, rows], dst_ref=ring_in.at[e, way, step, rows],
            send_sem=ring_send.at[e, way, step], recv_sem=ring_recv.at[e, way, step],
            device_id=up(1 - 2 * way), device_id_type=MESH,
        )

    @pl.loop(0, heads)
    def _(e):
        gath[e, me] = att_ref[e]
        for half in (0, 1):
            for slot, (leg, by) in enumerate(((0, 1), (0, -1), (1, 1), (1, -1))):
                put(e, half, me, None, leg, by, slot).start()

    send_weight().start()
    own_weight = pltpu.make_async_copy(w_ref, weight.at[core], w_local)
    own_weight.start()
    mixed_sum[...] = jnp.zeros_like(mixed_sum)
    own_weight.wait()

    def gather_first(e):
        for half in (0, 1):
            for by in (-1, 1):
                block = block_at(half, by, 0)
                arrived(e, half, block)
                base = 4 if by == -1 else 6
                put(e, half, block, 0 if by == -1 else 1, 0, -by, 10 if by == -1 else 11).start()
                put(e, half, block, None, 1, 1, base).start()
                put(e, half, block, None, 1, -1, base + 1).start()

    def gather_opposite(e):
        for half in (0, 1):
            block = block_at(half, 2, 0)
            arrived(e, half, block)
            put(e, half, block, None, 1, 1, 8).start()
            put(e, half, block, None, 1, -1, 9).start()

    def gather_line(e, first, at):
        for half in (0, 1):
            for by in (-1, 1):
                block = block_at(half, first, by)
                arrived(e, half, block)
                put(e, half, block, 0 if by == -1 else 1, 1, -by, 12 + 2 * at + (0 if by == -1 else 1)).start()

    def gather_rest(e):
        for half in (0, 1):
            for first in (0, -1, 1, 2):
                arrived(e, half, block_at(half, first, 2))

    def gradient_parts(e):
        for part in (0, 1):
            for_sibling = gath[e, pl.ds((1 - core) * DEPTH + part * 4, 4)].reshape(4 * HD, BLOCK)
            pair_out[e, pl.ds(part * 4, 4)] = (
                jnp.dot(for_sibling, cot_ref[...], preferred_element_type=jnp.float32)
                .astype(jnp.bfloat16).reshape(4, HD, cot_ref.shape[1])
            )
        send_pair(e).start()
        for part in (0, 1):
            for_me = gath[e, pl.ds(core * DEPTH + part * 4, 4)].reshape(4 * HD, BLOCK)
            kept[e, pl.ds(part * 4, 4)] = jnp.dot(
                for_me, cot_ref[...], preferred_element_type=jnp.float32
            ).reshape(4, HD, cot_ref.shape[1])

    def mix(e):
        @pl.loop(0, ROWS // 4)
        def _(part):
            blocks = gath[e, pl.ds(part * 4, 4)].reshape(4 * HD, BLOCK)
            matrix = weight[lax.div(part, 2), pl.ds(lax.rem(part, 2) * 4, 4), e].reshape(4 * HD, cot_ref.shape[1])
            mixed_sum[...] += lax.dot_general(
                blocks, matrix, (((0,), (0,)), ((), ())), preferred_element_type=jnp.float32
            )

    def chip_part(e, target):
        return kept[e, target] + pair_in[e, target].astype(jnp.float32)

    def ring_start(e):
        send_pair(e).wait_recv()
        for way in (0, 1):
            target = shifted(z, 4, DEPTH)
            rows = pl.ds(way * HALF, HALF)
            ring_out[e, way, 0, rows] = (
                kept[e, target, rows] + pair_in[e, target, rows].astype(jnp.float32)
            ).astype(jnp.bfloat16)
            send_ring(e, way, 0).start()

    def ring_step(e, step):
        for way in (0, 1):
            send_ring(e, way, step - 1).wait_recv()
            target = shifted(z, (4 - step) * (1 - 2 * way), DEPTH)
            for half in (0, 1):
                rows = pl.ds(half * HALF, HALF)
                total = kept[e, target, rows] + pair_in[e, target, rows].astype(jnp.float32)
                if step > 1 or half == way:
                    total += ring_in[e, way, step - 1, rows].astype(jnp.float32)
                ring_out[e, way, step, rows] = total.astype(jnp.bfloat16)
            send_ring(e, way, step).start()

    def ring_end(e):
        send_ring(e, 0, 3).wait_recv()
        send_ring(e, 1, 3).wait_recv()
        total = chip_part(e, z) + ring_in[e, 0, 3].astype(jnp.float32) + ring_in[e, 1, 3].astype(jnp.float32)
        grad_ref[e] = total.astype(jnp.bfloat16)

    @pl.loop(0, heads + 1)
    def _(it):
        gathers = it < heads
        reduces = it > 0
        e = jnp.minimum(it, heads - 1)
        b = jnp.maximum(it - 1, 0)
        pl.when(reduces)(lambda: gradient_parts(b))
        pl.when(gathers)(lambda: gather_first(e))
        pl.when(reduces)(lambda: ring_start(b))
        pl.when(gathers)(lambda: gather_opposite(e))
        pl.when(it == 1)(lambda: send_weight().wait_recv())
        pl.when(reduces)(lambda: mix(b))
        pl.when(gathers)(lambda: gather_line(e, 0, 0))
        pl.when(reduces)(lambda: ring_step(b, 1))
        pl.when(gathers)(lambda: gather_line(e, -1, 1))
        pl.when(reduces)(lambda: ring_step(b, 2))
        pl.when(gathers)(lambda: gather_line(e, 1, 2))
        pl.when(reduces)(lambda: ring_step(b, 3))
        pl.when(gathers)(lambda: gather_line(e, 2, 3))
        pl.when(gathers)(lambda: gather_rest(e))
        pl.when(reduces)(lambda: ring_end(b))

    mixed_ref[...] = mixed_sum[...].astype(jnp.bfloat16)

    send_weight().wait_send()

    @pl.loop(0, heads)
    def _(e):
        for half in (0, 1):
            @pl.loop(0, 10)
            def _(slot):
                put(e, half, me, None, 0, 1, slot).wait_send()

            @pl.loop(10, 20)
            def _(slot):
                put(e, half, me, 0, 0, 1, slot).wait_send()

        send_pair(e).wait_send()
        for way in (0, 1):
            for step in range(4):
                send_ring(e, way, step).wait_send()


def project(attended, weight_half, cotangent):
    heads = attended.shape[0]
    width = cotangent.shape[1]
    vmem = pl.BlockSpec(memory_space=pltpu.VMEM)
    dma = pltpu.SemaphoreType.DMA
    low = jnp.bfloat16
    return pl.pallas_call(
        project_kernel,
        out_shape=(
            jax.ShapeDtypeStruct((BLOCK, width), low),
            jax.ShapeDtypeStruct((heads, HD, width), low),
        ),
        in_specs=[vmem] * 3,
        out_specs=(vmem, vmem),
        scratch_shapes=[
            pltpu.VMEM((heads, ROWS, HD, BLOCK), low),
            pltpu.VMEM((2, ROWS // 2, heads, HD, width), low),
            pltpu.VMEM((BLOCK, width), jnp.float32),
            pltpu.VMEM((heads, DEPTH, HD, width), jnp.float32),
            pltpu.VMEM((heads, DEPTH, HD, width), low),
            pltpu.VMEM((heads, DEPTH, HD, width), low),
            pltpu.VMEM((heads, 2, 4, HD, width), low),
            pltpu.VMEM((heads, 2, 4, HD, width), low),
            dma((heads, 2, 20)), dma((heads, 2, ROWS)), dma, dma, dma,
            dma((heads,)), dma((heads,)), dma((heads, 2, 4)), dma((heads, 2, 4)),
        ],
        compiler_params=pltpu.CompilerParams(
            collective_id=1, has_side_effects=True, vmem_limit_bytes=56 << 20
        ),
    )(attended, weight_half, cotangent)


def body(queries, keys, values, out_weight, cotangent, block_mask):
    place = lax.axis_index(("col", "ctx"))
    width = queries.shape[1]
    mask_row = lax.dynamic_index_in_dim(block_mask, place, 0, keepdims=False)
    all_keys = lax.all_gather(keys, ("col", "ctx"), axis=0, tiled=True)
    all_values = lax.all_gather(values, ("col", "ctx"), axis=0, tiled=True)
    attended = attend(place.reshape(1), mask_row, queries, all_keys, all_values)
    mixed_out, grad_weight = project(
        attended, out_weight.reshape(ROWS // 2, width // HD, HD, width), cotangent
    )
    return (mixed_out, grad_weight.reshape(width, width))


def solution(mesh):
    tokens = P(("col", "ctx"), "row")
    return jax.shard_map(
        body,
        mesh=mesh,
        in_specs=(tokens, tokens, tokens, P("col", "row"), tokens, P()),
        out_specs=(tokens, tokens),
        check_vma=False,
    )
```

```python
import functools
import math

import jax
import jax.numpy as jnp
from jax import lax
from jax.experimental import pallas as pl
from jax.experimental.pallas import tpu as pltpu
from jax.sharding import PartitionSpec as P

HD = 128
BLOCK = 512
SIDE = 4
ROWS = SIDE * SIDE
DEPTH = 8
HALF = HD // 2
QUARTER = HD // 4
MESH = pl.DeviceIdType.MESH


def shifted(value, by, size):
    return lax.rem(value + (by + size), size)


def attend_kernel(
    mask_ref, q_ref, k_ref, v_ref, out_ref,
    queries, keys, values, run_max, run_sum, weighted, ring_send, ring_recv, pair_send, pair_recv,
):
    core = lax.axis_index("col")
    z = lax.axis_index("ctx")
    heads = out_ref.shape[0]
    rate = math.log2(math.e) / math.sqrt(HD)
    stores = (keys, values)
    is_key, is_value = 0, 1

    barrier = pltpu.get_barrier_semaphore()
    for by in (1, -1):
        pl.semaphore_signal(barrier, inc=1, device_id={"ctx": shifted(z, by, DEPTH)}, device_id_type=MESH)
    pl.semaphore_signal(barrier, inc=1, device_id={"col": 1 - core}, device_id_type=MESH)
    for e in range(heads):
        columns = slice(e * HD, (e + 1) * HD)
        keys[core, z, e] = k_ref[:, columns]
    pl.semaphore_wait(barrier, 3)

    def ring(kind, e, block, by):
        ref = stores[kind].at[core, block, e]
        way = 0 if by == 1 else 1
        return pltpu.make_async_remote_copy(
            src_ref=ref, dst_ref=ref, send_sem=ring_send.at[way, kind, block, e], recv_sem=ring_recv.at[kind, block, e],
            device_id={"ctx": shifted(z, by, DEPTH)}, device_id_type=MESH,
        )

    def pair(kind, e, block):
        ref = stores[kind].at[0, block, e]
        return pltpu.make_async_remote_copy(
            src_ref=ref, dst_ref=ref, send_sem=pair_send.at[kind, block, e], recv_sem=pair_recv.at[kind, block, e],
            device_id={"col": 1 - core}, device_id_type=MESH,
        )

    def hand_over(kind, e, block):
        pl.when(core == 0)(lambda: pair(kind, e, block).start())

    for kind in (is_key, is_value):
        for e in range(heads):
            if kind == is_value:
                values[core, z, e] = v_ref[:, e * HD:(e + 1) * HD].T
            ring(kind, e, z, 1).start()
            ring(kind, e, z, -1).start()
            hand_over(kind, e, z)

    for e in range(heads):
        queries[e] = q_ref[:, e * HD:(e + 1) * HD]
    run_max[...] = jnp.full_like(run_max, -1e30)
    run_sum[...] = jnp.zeros_like(run_sum)
    weighted[...] = jnp.zeros_like(weighted)

    def pass_on(hop):
        @pl.loop(0, heads)
        def _(e):
            for kind in (is_key, is_value):
                for by in (1, -1):
                    longer = (kind == is_key) == (by == 1)
                    if hop == 4 and not longer:
                        continue
                    block = shifted(z, -by * hop, DEPTH)
                    ring(kind, e, block, by).wait_recv()
                    if hop < 3 or (hop == 3 and longer):
                        ring(kind, e, block, by).start()
                    hand_over(kind, e, block)

    def absorb(e, group, blocks):
        row = core * DEPTH + z
        query = queries[e]
        parts = []
        new_max = run_max[e]
        for block in blocks:
            penalty = jnp.where(mask_ref[row, group * DEPTH + block] == 1, 0.0, 1e30)
            scores = lax.dot_general(
                keys[group, block, e], query, (((1,), (1,)), ((), ())), preferred_element_type=jnp.float32
            )
            new_max = jnp.maximum(new_max, jnp.max(scores, axis=0, keepdims=True) - penalty)
            parts.append((block, penalty, scores))
        correction = jnp.exp2((run_max[e] - new_max) * rate)
        total = run_sum[e] * correction
        product = weighted[e] * correction
        for block, penalty, scores in parts:
            probs = jnp.exp2(scores * rate - (new_max * rate + penalty))
            total += jnp.sum(probs, axis=0, keepdims=True)
            product += jnp.dot(
                values[group, block, e], probs.astype(jnp.bfloat16), preferred_element_type=jnp.float32
            )
        run_max[e] = new_max
        run_sum[e] = total
        weighted[e] = product

    def compute(hop):
        blocks = [shifted(z, by * hop, DEPTH) for by in ((1, -1) if 0 < hop < 4 else (1,))]

        @pl.loop(0, heads)
        def _(e):
            absorb(e, core, blocks)

            @pl.when(core == 1)
            def _():
                for block in blocks:
                    for kind in (is_key, is_value):
                        pair(kind, e, block).wait_recv()
                absorb(e, 0, blocks)

    for hop in range(1, 5):
        pass_on(hop)
        compute(hop - 1)
    compute(4)

    @pl.loop(0, heads)
    def _(e):
        out_ref[e] = (weighted[e] / run_sum[e]).astype(out_ref.dtype)

    @pl.loop(0, heads)
    def _(e):
        for kind in (is_key, is_value):
            for by in (1, -1):
                for hop in range(4 if (kind == is_key) == (by == 1) else 3):
                    ring(kind, e, shifted(z, -by * hop, DEPTH), by).wait_send()

            @pl.when(core == 0)
            def _():
                @pl.loop(0, DEPTH)
                def _(block):
                    pair(kind, e, block).wait_send()


def attend(block_mask, queries, keys, values):
    rows, width = queries.shape
    heads = width // HD
    vmem = pl.BlockSpec(memory_space=pltpu.VMEM)
    dma = pltpu.SemaphoreType.DMA
    return pl.pallas_call(
        attend_kernel,
        out_shape=jax.ShapeDtypeStruct((heads, HD, rows), jnp.bfloat16),
        in_specs=[pl.BlockSpec(memory_space=pltpu.SMEM), vmem, vmem, vmem],
        out_specs=vmem,
        scratch_shapes=[
            pltpu.VMEM((heads, BLOCK, HD), jnp.bfloat16),
            pltpu.VMEM((2, DEPTH, heads, BLOCK, HD), jnp.bfloat16),
            pltpu.VMEM((2, DEPTH, heads, HD, BLOCK), jnp.bfloat16),
            pltpu.VMEM((heads, 1, BLOCK), jnp.float32),
            pltpu.VMEM((heads, 1, BLOCK), jnp.float32),
            pltpu.VMEM((heads, HD, BLOCK), jnp.float32),
            dma((2, 2, DEPTH, heads)), dma((2, DEPTH, heads)), dma((2, DEPTH, heads)), dma((2, DEPTH, heads)),
        ],
        compiler_params=pltpu.CompilerParams(
            collective_id=0, has_side_effects=True, vmem_limit_bytes=56 << 20
        ),
    )(block_mask, queries, keys, values)


def project_kernel(
    att_ref, w_ref, cot_ref, mixed_ref, grad_ref,
    gath, weight, mixed_sum, kept, pair_out, pair_in, ring_out, ring_in,
    ag_send, ag_recv, w_send, w_recv, w_local, pair_send, pair_recv, ring_send, ring_recv,
):
    me = lax.axis_index("row")
    core = lax.axis_index("col")
    z = lax.axis_index("ctx")
    here = (lax.rem(me, SIDE), lax.div(me, SIDE))
    heads = att_ref.shape[0]

    def block_at(half, first, second):
        by = (first, second) if half == 0 else (second, first)
        return shifted(here[1], by[1], SIDE) * SIDE + shifted(here[0], by[0], SIDE)

    def up(by):
        return {"ctx": shifted(z, by, DEPTH)}

    sibling = {"col": 1 - core}

    barrier = pltpu.get_barrier_semaphore()
    for first, second in ((1, 0), (-1, 0), (0, 1), (0, -1)):
        pl.semaphore_signal(barrier, inc=1, device_id={"row": block_at(0, first, second)}, device_id_type=MESH)
    for by in (1, -1):
        pl.semaphore_signal(barrier, inc=1, device_id=up(by), device_id_type=MESH)
    pl.semaphore_signal(barrier, inc=1, device_id=sibling, device_id_type=MESH)
    pl.semaphore_wait(barrier, 7)

    def put(e, half, block, quarter, leg, by, slot):
        low = half * HALF + (0 if quarter is None else quarter * QUARTER)
        ref = gath.at[e, block, pl.ds(low, HALF if quarter is None else QUARTER)]
        to = block_at(half, by, 0) if leg == 0 else block_at(half, 0, by)
        return pltpu.make_async_remote_copy(
            src_ref=ref, dst_ref=ref, send_sem=ag_send.at[e, half, slot], recv_sem=ag_recv.at[e, half, block],
            device_id={"row": to}, device_id_type=MESH,
        )

    def arrived(e, half, block):
        put(e, half, block, None, 0, 1, 0).wait_recv()

    def send_weight():
        return pltpu.make_async_remote_copy(
            src_ref=w_ref, dst_ref=weight.at[core], send_sem=w_send, recv_sem=w_recv,
            device_id=sibling, device_id_type=MESH,
        )

    def send_pair(e):
        return pltpu.make_async_remote_copy(
            src_ref=pair_out.at[e], dst_ref=pair_in.at[e], send_sem=pair_send.at[e], recv_sem=pair_recv.at[e],
            device_id=sibling, device_id_type=MESH,
        )

    def send_ring(e, way, step):
        rows = pl.ds(way * HALF, HALF) if step == 0 else pl.ds(0, HD)
        return pltpu.make_async_remote_copy(
            src_ref=ring_out.at[e, way, step, rows], dst_ref=ring_in.at[e, way, step, rows],
            send_sem=ring_send.at[e, way, step], recv_sem=ring_recv.at[e, way, step],
            device_id=up(1 - 2 * way), device_id_type=MESH,
        )

    @pl.loop(0, heads)
    def _(e):
        gath[e, me] = att_ref[e]
        for half in (0, 1):
            for slot, (leg, by) in enumerate(((0, 1), (0, -1), (1, 1), (1, -1))):
                put(e, half, me, None, leg, by, slot).start()

    send_weight().start()
    own_weight = pltpu.make_async_copy(w_ref, weight.at[core], w_local)
    own_weight.start()
    mixed_sum[...] = jnp.zeros_like(mixed_sum)
    own_weight.wait()

    def gather_first(e):
        for half in (0, 1):
            for by in (-1, 1):
                block = block_at(half, by, 0)
                arrived(e, half, block)
                base = 4 if by == -1 else 6
                put(e, half, block, 0 if by == -1 else 1, 0, -by, 10 if by == -1 else 11).start()
                put(e, half, block, None, 1, 1, base).start()
                put(e, half, block, None, 1, -1, base + 1).start()

    def gather_opposite(e):
        for half in (0, 1):
            block = block_at(half, 2, 0)
            arrived(e, half, block)
            put(e, half, block, None, 1, 1, 8).start()
            put(e, half, block, None, 1, -1, 9).start()

    def gather_line(e, first, at):
        for half in (0, 1):
            for by in (-1, 1):
                block = block_at(half, first, by)
                arrived(e, half, block)
                put(e, half, block, 0 if by == -1 else 1, 1, -by, 12 + 2 * at + (0 if by == -1 else 1)).start()

    def gather_rest(e):
        for half in (0, 1):
            for first in (0, -1, 1, 2):
                arrived(e, half, block_at(half, first, 2))

    def gradient_parts(e):
        for part in (0, 1):
            for_sibling = gath[e, pl.ds((1 - core) * DEPTH + part * 4, 4)].reshape(4 * HD, BLOCK)
            pair_out[e, pl.ds(part * 4, 4)] = (
                jnp.dot(for_sibling, cot_ref[...], preferred_element_type=jnp.float32)
                .astype(jnp.bfloat16).reshape(4, HD, cot_ref.shape[1])
            )
        send_pair(e).start()
        for part in (0, 1):
            for_me = gath[e, pl.ds(core * DEPTH + part * 4, 4)].reshape(4 * HD, BLOCK)
            kept[e, pl.ds(part * 4, 4)] = jnp.dot(
                for_me, cot_ref[...], preferred_element_type=jnp.float32
            ).reshape(4, HD, cot_ref.shape[1])

    def mix(e):
        @pl.loop(0, ROWS // 4)
        def _(part):
            blocks = gath[e, pl.ds(part * 4, 4)].reshape(4 * HD, BLOCK)
            matrix = weight[lax.div(part, 2), pl.ds(lax.rem(part, 2) * 4, 4), e].reshape(4 * HD, cot_ref.shape[1])
            mixed_sum[...] += lax.dot_general(
                blocks, matrix, (((0,), (0,)), ((), ())), preferred_element_type=jnp.float32
            )

    def chip_part(e, target):
        return kept[e, target] + pair_in[e, target].astype(jnp.float32)

    def ring_start(e):
        send_pair(e).wait_recv()
        for way in (0, 1):
            target = shifted(z, 4, DEPTH)
            rows = pl.ds(way * HALF, HALF)
            ring_out[e, way, 0, rows] = (
                kept[e, target, rows] + pair_in[e, target, rows].astype(jnp.float32)
            ).astype(jnp.bfloat16)
            send_ring(e, way, 0).start()

    def ring_step(e, step):
        for way in (0, 1):
            send_ring(e, way, step - 1).wait_recv()
            target = shifted(z, (4 - step) * (1 - 2 * way), DEPTH)
            for half in (0, 1):
                rows = pl.ds(half * HALF, HALF)
                total = kept[e, target, rows] + pair_in[e, target, rows].astype(jnp.float32)
                if step > 1 or half == way:
                    total += ring_in[e, way, step - 1, rows].astype(jnp.float32)
                ring_out[e, way, step, rows] = total.astype(jnp.bfloat16)
            send_ring(e, way, step).start()

    def ring_end(e):
        send_ring(e, 0, 3).wait_recv()
        send_ring(e, 1, 3).wait_recv()
        total = chip_part(e, z) + ring_in[e, 0, 3].astype(jnp.float32) + ring_in[e, 1, 3].astype(jnp.float32)
        grad_ref[e] = total.astype(jnp.bfloat16)

    @pl.loop(0, heads + 1)
    def _(it):
        gathers = it < heads
        reduces = it > 0
        e = jnp.minimum(it, heads - 1)
        b = jnp.maximum(it - 1, 0)
        pl.when(reduces)(lambda: gradient_parts(b))
        pl.when(gathers)(lambda: gather_first(e))
        pl.when(reduces)(lambda: ring_start(b))
        pl.when(gathers)(lambda: gather_opposite(e))
        pl.when(it == 1)(lambda: send_weight().wait_recv())
        pl.when(reduces)(lambda: mix(b))
        pl.when(gathers)(lambda: gather_line(e, 0, 0))
        pl.when(reduces)(lambda: ring_step(b, 1))
        pl.when(gathers)(lambda: gather_line(e, -1, 1))
        pl.when(reduces)(lambda: ring_step(b, 2))
        pl.when(gathers)(lambda: gather_line(e, 1, 2))
        pl.when(reduces)(lambda: ring_step(b, 3))
        pl.when(gathers)(lambda: gather_line(e, 2, 3))
        pl.when(gathers)(lambda: gather_rest(e))
        pl.when(reduces)(lambda: ring_end(b))

    mixed_ref[...] = mixed_sum[...].astype(jnp.bfloat16)

    send_weight().wait_send()

    @pl.loop(0, heads)
    def _(e):
        for half in (0, 1):
            @pl.loop(0, 10)
            def _(slot):
                put(e, half, me, None, 0, 1, slot).wait_send()

            @pl.loop(10, 20)
            def _(slot):
                put(e, half, me, 0, 0, 1, slot).wait_send()

        send_pair(e).wait_send()
        for way in (0, 1):
            for step in range(4):
                send_ring(e, way, step).wait_send()


def project(attended, weight_half, cotangent):
    heads = attended.shape[0]
    width = cotangent.shape[1]
    vmem = pl.BlockSpec(memory_space=pltpu.VMEM)
    dma = pltpu.SemaphoreType.DMA
    low = jnp.bfloat16
    return pl.pallas_call(
        project_kernel,
        out_shape=(
            jax.ShapeDtypeStruct((BLOCK, width), low),
            jax.ShapeDtypeStruct((heads, HD, width), low),
        ),
        in_specs=[vmem] * 3,
        out_specs=(vmem, vmem),
        scratch_shapes=[
            pltpu.VMEM((heads, ROWS, HD, BLOCK), low),
            pltpu.VMEM((2, ROWS // 2, heads, HD, width), low),
            pltpu.VMEM((BLOCK, width), jnp.float32),
            pltpu.VMEM((heads, DEPTH, HD, width), jnp.float32),
            pltpu.VMEM((heads, DEPTH, HD, width), low),
            pltpu.VMEM((heads, DEPTH, HD, width), low),
            pltpu.VMEM((heads, 2, 4, HD, width), low),
            pltpu.VMEM((heads, 2, 4, HD, width), low),
            dma((heads, 2, 20)), dma((heads, 2, ROWS)), dma, dma, dma,
            dma((heads,)), dma((heads,)), dma((heads, 2, 4)), dma((heads, 2, 4)),
        ],
        compiler_params=pltpu.CompilerParams(
            collective_id=1, has_side_effects=True, vmem_limit_bytes=56 << 20
        ),
    )(attended, weight_half, cotangent)


def body(queries, keys, values, out_weight, cotangent, block_mask):
    width = queries.shape[1]
    attended = attend(block_mask, queries, keys, values)
    mixed_out, grad_weight = project(
        attended, out_weight.reshape(ROWS // 2, width // HD, HD, width), cotangent
    )
    return (mixed_out, grad_weight.reshape(width, width))


def solution(mesh):
    tokens = P(("col", "ctx"), "row")
    return jax.shard_map(
        body,
        mesh=mesh,
        in_specs=(tokens, tokens, tokens, P("col", "row"), tokens, P()),
        out_specs=(tokens, tokens),
        check_vma=False,
    )
```

```python
import functools
import math

import jax
import jax.numpy as jnp
from jax import lax
from jax.experimental import pallas as pl
from jax.experimental.pallas import tpu as pltpu
from jax.sharding import PartitionSpec as P

HD = 128
BLOCK = 512
SIDE = 4
ROWS = SIDE * SIDE
DEPTH = 8
HALF = HD // 2
QUARTER = HD // 4
MESH = pl.DeviceIdType.MESH


def shifted(value, by, size):
    return lax.rem(value + (by + size), size)


def layer_kernel(
    mask_ref, q_ref, k_ref, v_ref, w_ref, cot_ref, mixed_ref, grad_ref,
    queries, keys, values, run_max, run_sum, weighted,
    gath, weight, cot, mixed_sum, kept, pair_out, pair_in, ring_out, ring_in,
    kv_send, kv_recv, hand_send, hand_recv, ag_send, ag_recv,
    w_send, w_recv, local, pair_send, pair_recv, ring_send, ring_recv,
):
    me = lax.axis_index("row")
    core = lax.axis_index("col")
    z = lax.axis_index("ctx")
    here = (lax.rem(me, SIDE), lax.div(me, SIDE))
    heads = grad_ref.shape[0]
    width = cot_ref.shape[1]
    rate = math.log2(math.e) / math.sqrt(HD)
    stores = (keys, values)
    is_key, is_value = 0, 1
    sibling = {"col": 1 - core}

    def up(by):
        return {"ctx": shifted(z, by, DEPTH)}

    def block_at(half, first, second):
        by = (first, second) if half == 0 else (second, first)
        return shifted(here[1], by[1], SIDE) * SIDE + shifted(here[0], by[0], SIDE)

    fetch_weight = pltpu.make_async_copy(w_ref, weight.at[core], local.at[0])
    fetch_cot = pltpu.make_async_copy(cot_ref, cot, local.at[1])

    barrier = pltpu.get_barrier_semaphore()
    for first, second in ((1, 0), (-1, 0), (2, 0), (0, 1), (0, -1), (0, 2)):
        pl.semaphore_signal(barrier, inc=1, device_id={"row": block_at(0, first, second)}, device_id_type=MESH)
    for by in (1, -1):
        pl.semaphore_signal(barrier, inc=1, device_id=up(by), device_id_type=MESH)
    pl.semaphore_signal(barrier, inc=1, device_id=sibling, device_id_type=MESH)
    fetch_weight.start()
    fetch_cot.start()
    for e in range(heads):
        keys[core, z, e] = k_ref[:, e * HD:(e + 1) * HD]
    pl.semaphore_wait(barrier, 9)

    def kv(kind, e, block, by):
        ref = stores[kind].at[core, block, e]
        way = 0 if by == 1 else 1
        return pltpu.make_async_remote_copy(
            src_ref=ref, dst_ref=ref, send_sem=kv_send.at[way, kind, block, e], recv_sem=kv_recv.at[kind, block, e],
            device_id=up(by), device_id_type=MESH,
        )

    def hand(kind, e, block):
        ref = stores[kind].at[0, block, e]
        return pltpu.make_async_remote_copy(
            src_ref=ref, dst_ref=ref, send_sem=hand_send.at[kind, block, e], recv_sem=hand_recv.at[kind, block, e],
            device_id=sibling, device_id_type=MESH,
        )

    def hand_over(kind, e, block):
        pl.when(core == 0)(lambda: hand(kind, e, block).start())

    def kv_own(e):
        for kind in (is_key, is_value):
            if kind == is_value:
                values[core, z, e] = v_ref[:, e * HD:(e + 1) * HD].T
            kv(kind, e, z, 1).start()
            kv(kind, e, z, -1).start()
            hand_over(kind, e, z)

    def kv_pass(e, hop):
        for kind in (is_key, is_value):
            for by in (1, -1):
                longer = (kind == is_key) == (by == 1)
                if hop == 4 and not longer:
                    continue
                block = shifted(z, -by * hop, DEPTH)
                kv(kind, e, block, by).wait_recv()
                if hop < 3 or (hop == 3 and longer):
                    kv(kind, e, block, by).start()
                hand_over(kind, e, block)

    def absorb(e, group, blocks):
        row = core * DEPTH + z
        query = queries[e]
        parts = []
        new_max = run_max[e]
        for block in blocks:
            penalty = jnp.where(mask_ref[row, group * DEPTH + block] == 1, 0.0, 1e30)
            scores = lax.dot_general(
                keys[group, block, e], query, (((1,), (1,)), ((), ())), preferred_element_type=jnp.float32
            )
            new_max = jnp.maximum(new_max, jnp.max(scores, axis=0, keepdims=True) - penalty)
            parts.append((block, penalty, scores))
        correction = jnp.exp2((run_max[e] - new_max) * rate)
        total = run_sum[e] * correction
        product = weighted[e] * correction
        for block, penalty, scores in parts:
            probs = jnp.exp2(scores * rate - (new_max * rate + penalty))
            total += jnp.sum(probs, axis=0, keepdims=True)
            product += jnp.dot(
                values[group, block, e], probs.astype(jnp.bfloat16), preferred_element_type=jnp.float32
            )
        run_max[e] = new_max
        run_sum[e] = total
        weighted[e] = product

    def compute(e, hop):
        blocks = [shifted(z, by * hop, DEPTH) for by in ((1, -1) if 0 < hop < 4 else (1,))]

        @pl.loop(0, 1 + core)
        def _(turn):
            @pl.when(turn == 1)
            def _():
                for block in blocks:
                    for kind in (is_key, is_value):
                        hand(kind, e, block).wait_recv()
            absorb(e, core - turn, blocks)

    def put(e, half, block, quarter, leg, by, slot):
        low = half * HALF + (0 if quarter is None else quarter * QUARTER)
        ref = gath.at[e, block, pl.ds(low, HALF if quarter is None else QUARTER)]
        to = block_at(half, by, 0) if leg == 0 else block_at(half, 0, by)
        return pltpu.make_async_remote_copy(
            src_ref=ref, dst_ref=ref, send_sem=ag_send.at[e, half, slot], recv_sem=ag_recv.at[e, half, block],
            device_id={"row": to}, device_id_type=MESH,
        )

    def arrived(e, half, block):
        put(e, half, block, None, 0, 1, 0).wait_recv()

    def gather_own(e):
        gath[e, me] = (weighted[e] / run_sum[e]).astype(gath.dtype)
        for slot, (leg, by) in enumerate(((0, 1), (0, -1), (0, 2), (1, 1), (1, -1))):
            for half in (0, 1):
                put(e, half, me, None, leg, by, slot).start()

    def gather_first(e, by):
        for half in (0, 1):
            block = block_at(half, by, 0)
            arrived(e, half, block)
            base = {-1: 5, 1: 7, 2: 9}[by]
            put(e, half, block, None, 1, 1, base).start()
            put(e, half, block, None, 1, -1, base + 1).start()

    def gather_line(e, first):
        at = {0: 11, -1: 13, 1: 15, 2: 17}[first]
        for half in (0, 1):
            for by in (-1, 1):
                block = block_at(half, first, by)
                arrived(e, half, block)
                quarter = 0 if by == -1 else 1
                put(e, half, block, quarter, 1, -by, at + quarter).start()

    def gather_rest(e):
        for half in (0, 1):
            for first in (0, -1, 1, 2):
                arrived(e, half, block_at(half, first, 2))

    def send_weight():
        return pltpu.make_async_remote_copy(
            src_ref=weight.at[core], dst_ref=weight.at[core], send_sem=w_send, recv_sem=w_recv,
            device_id=sibling, device_id_type=MESH,
        )

    def send_pair(e):
        return pltpu.make_async_remote_copy(
            src_ref=pair_out.at[e], dst_ref=pair_in.at[e], send_sem=pair_send.at[e], recv_sem=pair_recv.at[e],
            device_id=sibling, device_id_type=MESH,
        )

    def send_ring(e, way, step):
        rows = pl.ds(way * HALF, HALF) if step == 0 else pl.ds(0, HD)
        return pltpu.make_async_remote_copy(
            src_ref=ring_out.at[e, way, step, rows], dst_ref=ring_in.at[e, way, step, rows],
            send_sem=ring_send.at[e, way, step], recv_sem=ring_recv.at[e, way, step],
            device_id=up(1 - 2 * way), device_id_type=MESH,
        )

    def gradient_parts(e):
        @pl.loop(0, 2)
        def _(part):
            blocks = gath[e, pl.ds((1 - core) * DEPTH + part * 4, 4)].reshape(4 * HD, BLOCK)
            pair_out[e, pl.ds(part * 4, 4)] = (
                jnp.dot(blocks, cot[...], preferred_element_type=jnp.float32)
                .astype(jnp.bfloat16).reshape(4, HD, width)
            )
        send_pair(e).start()

        @pl.loop(0, 2)
        def _(part):
            blocks = gath[e, pl.ds(core * DEPTH + part * 4, 4)].reshape(4 * HD, BLOCK)
            kept[e, pl.ds(part * 4, 4)] = jnp.dot(
                blocks, cot[...], preferred_element_type=jnp.float32
            ).reshape(4, HD, width)

    def mix(e):
        @pl.loop(0, ROWS // 4)
        def _(part):
            blocks = gath[e, pl.ds(part * 4, 4)].reshape(4 * HD, BLOCK)
            matrix = weight[lax.div(part, 2), pl.ds(lax.rem(part, 2) * 4, 4), e].reshape(4 * HD, width)
            mixed_sum[...] += lax.dot_general(
                blocks, matrix, (((0,), (0,)), ((), ())), preferred_element_type=jnp.float32
            )

    def ring_start(e):
        send_pair(e).wait_recv()
        for way in (0, 1):
            target = shifted(z, 4, DEPTH)
            rows = pl.ds(way * HALF, HALF)
            ring_out[e, way, 0, rows] = (
                kept[e, target, rows] + pair_in[e, target, rows].astype(jnp.float32)
            ).astype(jnp.bfloat16)
            send_ring(e, way, 0).start()

    def ring_step(e, step):
        for way in (0, 1):
            send_ring(e, way, step - 1).wait_recv()
            target = shifted(z, (4 - step) * (1 - 2 * way), DEPTH)
            for half in (0, 1):
                rows = pl.ds(half * HALF, HALF)
                total = kept[e, target, rows] + pair_in[e, target, rows].astype(jnp.float32)
                if step > 1 or half == way:
                    total += ring_in[e, way, step - 1, rows].astype(jnp.float32)
                ring_out[e, way, step, rows] = total.astype(jnp.bfloat16)
            send_ring(e, way, step).start()

    def ring_end(e):
        send_ring(e, 0, 3).wait_recv()
        send_ring(e, 1, 3).wait_recv()
        total = kept[e, z] + pair_in[e, z].astype(jnp.float32)
        total += ring_in[e, 0, 3].astype(jnp.float32) + ring_in[e, 1, 3].astype(jnp.float32)
        grad_ref[e] = total.astype(jnp.bfloat16)

    kv_own(0)
    kv_own(1)
    for e in range(heads):
        queries[e] = q_ref[:, e * HD:(e + 1) * HD]
    run_max[...] = jnp.full_like(run_max, -1e30)
    run_sum[...] = jnp.zeros_like(run_sum)
    weighted[...] = jnp.zeros_like(weighted)
    mixed_sum[...] = jnp.zeros_like(mixed_sum)
    fetch_weight.wait()
    fetch_cot.wait()
    send_weight().start()

    compute(0, 0)
    kv_pass(0, 1)
    compute(1, 0)
    kv_pass(1, 1)
    compute(0, 1)
    kv_pass(0, 2)
    kv_own(2)
    compute(1, 1)
    kv_pass(1, 2)
    compute(0, 2)
    kv_pass(0, 3)
    compute(2, 0)
    kv_pass(2, 1)
    compute(0, 3)
    kv_pass(0, 4)
    compute(0, 4)
    gather_own(0)
    kv_pass(1, 3)
    compute(1, 2)
    gather_first(0, -1)
    gather_first(0, 1)
    gather_first(0, 2)
    kv_pass(2, 2)
    compute(1, 3)
    kv_pass(1, 4)
    compute(1, 4)
    gather_own(1)
    gather_line(0, 0)
    gather_line(0, -1)
    kv_pass(2, 3)
    compute(2, 1)
    gather_line(0, 1)
    gather_line(0, 2)
    gather_first(1, -1)
    gather_first(1, 1)
    gather_first(1, 2)
    compute(2, 2)
    kv_pass(2, 4)
    gather_rest(0)
    compute(2, 3)
    compute(2, 4)
    gather_own(2)
    gather_line(1, 0)
    gather_line(1, -1)
    gather_line(1, 1)
    gather_line(1, 2)
    gradient_parts(0)
    gather_first(2, -1)
    gather_first(2, 1)
    gather_first(2, 2)
    ring_start(0)
    gather_rest(1)
    gradient_parts(1)
    ring_step(0, 1)
    gather_line(2, 0)
    ring_start(1)
    ring_step(0, 2)
    gather_line(2, -1)
    ring_step(1, 1)
    ring_step(0, 3)
    gather_line(2, 1)
    ring_step(1, 2)
    ring_end(0)
    gather_line(2, 2)
    ring_step(1, 3)
    send_weight().wait_recv()
    mix(0)
    gather_rest(2)
    gradient_parts(2)
    ring_start(2)
    ring_end(1)
    mix(1)
    ring_step(2, 1)
    mix(2)
    ring_step(2, 2)
    mixed_ref[...] = mixed_sum[...].astype(jnp.bfloat16)
    ring_step(2, 3)
    ring_end(2)

    send_weight().wait_send()

    @pl.loop(0, heads)
    def _(e):
        for kind in (is_key, is_value):
            for by in (1, -1):
                for hop in range(4 if (kind == is_key) == (by == 1) else 3):
                    kv(kind, e, shifted(z, -by * hop, DEPTH), by).wait_send()

            @pl.when(core == 0)
            def _():
                @pl.loop(0, DEPTH)
                def _(block):
                    hand(kind, e, block).wait_send()

        for half in (0, 1):
            @pl.loop(0, 11)
            def _(slot):
                put(e, half, me, None, 0, 1, slot).wait_send()

            @pl.loop(11, 19)
            def _(slot):
                put(e, half, me, 0, 0, 1, slot).wait_send()

        send_pair(e).wait_send()
        for way in (0, 1):
            for step in range(4):
                send_ring(e, way, step).wait_send()


def layer(block_mask, queries, keys, values, weight_half, cotangent):
    rows, width = queries.shape
    heads = width // HD
    vmem = pl.BlockSpec(memory_space=pltpu.VMEM)
    anywhere = pl.BlockSpec(memory_space=pl.ANY)
    dma = pltpu.SemaphoreType.DMA
    low, wide = jnp.bfloat16, jnp.float32
    return pl.pallas_call(
        layer_kernel,
        out_shape=(
            jax.ShapeDtypeStruct((rows, width), low),
            jax.ShapeDtypeStruct((heads, HD, width), low),
        ),
        in_specs=[pl.BlockSpec(memory_space=pltpu.SMEM), vmem, vmem, vmem, anywhere, anywhere],
        out_specs=(vmem, vmem),
        scratch_shapes=[
            pltpu.VMEM((heads, BLOCK, HD), low),
            pltpu.VMEM((2, DEPTH, heads, BLOCK, HD), low),
            pltpu.VMEM((2, DEPTH, heads, HD, BLOCK), low),
            pltpu.VMEM((heads, 1, BLOCK), wide),
            pltpu.VMEM((heads, 1, BLOCK), wide),
            pltpu.VMEM((heads, HD, BLOCK), wide),
            pltpu.VMEM((heads, ROWS, HD, BLOCK), low),
            pltpu.VMEM((2, ROWS // 2, heads, HD, width), low),
            pltpu.VMEM((BLOCK, width), low),
            pltpu.VMEM((BLOCK, width), wide),
            pltpu.VMEM((heads, DEPTH, HD, width), wide),
            pltpu.VMEM((heads, DEPTH, HD, width), low),
            pltpu.VMEM((heads, DEPTH, HD, width), low),
            pltpu.VMEM((heads, 2, 4, HD, width), low),
            pltpu.VMEM((heads, 2, 4, HD, width), low),
            dma((2, 2, DEPTH, heads)), dma((2, DEPTH, heads)), dma((2, DEPTH, heads)), dma((2, DEPTH, heads)),
            dma((heads, 2, 19)), dma((heads, 2, ROWS)), dma, dma, dma((2,)),
            dma((heads,)), dma((heads,)), dma((heads, 2, 4)), dma((heads, 2, 4)),
        ],
        compiler_params=pltpu.CompilerParams(
            collective_id=0, has_side_effects=True, vmem_limit_bytes=58 << 20
        ),
    )(block_mask, queries, keys, values, weight_half, cotangent)


def body(queries, keys, values, out_weight, cotangent, block_mask):
    width = queries.shape[1]
    mixed_out, grad_weight = layer(
        block_mask, queries, keys, values, out_weight.reshape(ROWS // 2, width // HD, HD, width), cotangent
    )
    return (mixed_out, grad_weight.reshape(width, width))


def solution(mesh):
    tokens = P(("col", "ctx"), "row")
    return jax.shard_map(
        body,
        mesh=mesh,
        in_specs=(tokens, tokens, tokens, P("col", "row"), tokens, P()),
        out_specs=(tokens, tokens),
        check_vma=False,
    )
```

```python
import functools
import math

import jax
import jax.numpy as jnp
from jax import lax
from jax.experimental import pallas as pl
from jax.experimental.pallas import tpu as pltpu
from jax.sharding import PartitionSpec as P

HD = 128
BLOCK = 512
SIDE = 4
ROWS = SIDE * SIDE
DEPTH = 8
HALF = HD // 2
QUARTER = HD // 4
MESH = pl.DeviceIdType.MESH


def shifted(value, by, size):
    return lax.rem(value + (by + size), size)


def layer_kernel(
    mask_ref, q_ref, k_ref, v_ref, w_ref, cot_ref, mixed_ref, grad_ref,
    queries, keys, values, run_max, run_sum, weighted,
    gath, weight, cot, mixed_sum, kept, pair_out, pair_in, ring_out, ring_in,
    kv_send, kv_recv, hand_send, hand_recv, ag_send, ag_recv,
    w_send, w_recv, local, pair_send, pair_recv, ring_send, ring_recv,
):
    me = lax.axis_index("row")
    core = lax.axis_index("col")
    z = lax.axis_index("ctx")
    here = (lax.rem(me, SIDE), lax.div(me, SIDE))
    heads = grad_ref.shape[0]
    width = cot_ref.shape[1]
    rate = math.log2(math.e) / math.sqrt(HD)
    stores = (keys, values)
    is_key, is_value = 0, 1
    sibling = {"col": 1 - core}

    def up(by):
        return {"ctx": shifted(z, by, DEPTH)}

    def block_at(half, first, second):
        by = (first, second) if half == 0 else (second, first)
        return shifted(here[1], by[1], SIDE) * SIDE + shifted(here[0], by[0], SIDE)

    fetch_weight = pltpu.make_async_copy(w_ref, weight.at[core], local.at[0])
    fetch_cot = pltpu.make_async_copy(cot_ref, cot, local.at[1])

    barrier = pltpu.get_barrier_semaphore()
    for first, second in ((1, 0), (-1, 0), (2, 0), (0, 1), (0, -1), (0, 2)):
        pl.semaphore_signal(barrier, inc=1, device_id={"row": block_at(0, first, second)}, device_id_type=MESH)
    for by in (1, -1):
        pl.semaphore_signal(barrier, inc=1, device_id=up(by), device_id_type=MESH)
    pl.semaphore_signal(barrier, inc=1, device_id=sibling, device_id_type=MESH)
    fetch_weight.start()
    fetch_cot.start()
    for e in range(heads):
        keys[core, z, e] = k_ref[:, e * HD:(e + 1) * HD]
    pl.semaphore_wait(barrier, 9)

    def kv(kind, e, block, by):
        ref = stores[kind].at[core, block, e]
        way = 0 if by == 1 else 1
        return pltpu.make_async_remote_copy(
            src_ref=ref, dst_ref=ref, send_sem=kv_send.at[way, kind, block, e], recv_sem=kv_recv.at[kind, block, e],
            device_id=up(by), device_id_type=MESH,
        )

    def hand(kind, e, block):
        ref = stores[kind].at[0, block, e]
        return pltpu.make_async_remote_copy(
            src_ref=ref, dst_ref=ref, send_sem=hand_send.at[kind, block, e], recv_sem=hand_recv.at[kind, block, e],
            device_id=sibling, device_id_type=MESH,
        )

    def hand_over(kind, e, block):
        pl.when(core == 0)(lambda: hand(kind, e, block).start())

    def kv_own(e, kinds=(0, 1)):
        for kind in kinds:
            if kind == is_value:
                values[core, z, e] = v_ref[:, e * HD:(e + 1) * HD].T
            kv(kind, e, z, 1).start()
            kv(kind, e, z, -1).start()
            hand_over(kind, e, z)

    def kv_pass(e, hop, kinds=(0, 1)):
        for kind in kinds:
            for by in (1, -1):
                longer = (kind == is_key) == (by == 1)
                if hop == 4 and not longer:
                    continue
                block = shifted(z, -by * hop, DEPTH)
                kv(kind, e, block, by).wait_recv()
                if hop < 3 or (hop == 3 and longer):
                    kv(kind, e, block, by).start()
                hand_over(kind, e, block)

    def absorb(e, group, blocks):
        row = core * DEPTH + z
        query = queries[e]
        parts = []
        new_max = run_max[e]
        for block in blocks:
            penalty = jnp.where(mask_ref[row, group * DEPTH + block] == 1, 0.0, 1e30)
            scores = lax.dot_general(
                keys[group, block, e], query, (((1,), (1,)), ((), ())), preferred_element_type=jnp.float32
            )
            new_max = jnp.maximum(new_max, jnp.max(scores, axis=0, keepdims=True) - penalty)
            parts.append((block, penalty, scores))
        correction = jnp.exp2((run_max[e] - new_max) * rate)
        total = run_sum[e] * correction
        product = weighted[e] * correction
        for block, penalty, scores in parts:
            probs = jnp.exp2(scores * rate - (new_max * rate + penalty))
            total += jnp.sum(probs, axis=0, keepdims=True)
            product += jnp.dot(
                values[group, block, e], probs.astype(jnp.bfloat16), preferred_element_type=jnp.float32
            )
        run_max[e] = new_max
        run_sum[e] = total
        weighted[e] = product

    def compute(e, hop):
        blocks = [shifted(z, by * hop, DEPTH) for by in ((1, -1) if 0 < hop < 4 else (1,))]

        @pl.loop(0, 1 + core)
        def _(turn):
            @pl.when(turn == 1)
            def _():
                for block in blocks:
                    for kind in (is_key, is_value):
                        hand(kind, e, block).wait_recv()
            absorb(e, core - turn, blocks)

    def put(e, half, block, quarter, leg, by, slot):
        low = half * HALF + (0 if quarter is None else quarter * QUARTER)
        ref = gath.at[e, block, pl.ds(low, HALF if quarter is None else QUARTER)]
        to = block_at(half, by, 0) if leg == 0 else block_at(half, 0, by)
        return pltpu.make_async_remote_copy(
            src_ref=ref, dst_ref=ref, send_sem=ag_send.at[e, half, slot], recv_sem=ag_recv.at[e, half, block],
            device_id={"row": to}, device_id_type=MESH,
        )

    def arrived(e, half, block):
        put(e, half, block, None, 0, 1, 0).wait_recv()

    def gather_own(e):
        gath[e, me] = (weighted[e] / run_sum[e]).astype(gath.dtype)
        for slot, (leg, by) in enumerate(((0, 1), (0, -1), (0, 2), (1, 1), (1, -1))):
            for half in (0, 1):
                put(e, half, me, None, leg, by, slot).start()

    def gather_first(e, by):
        for half in (0, 1):
            block = block_at(half, by, 0)
            arrived(e, half, block)
            base = {-1: 5, 1: 7, 2: 9}[by]
            put(e, half, block, None, 1, 1, base).start()
            put(e, half, block, None, 1, -1, base + 1).start()

    def gather_line(e, first):
        at = {0: 11, -1: 13, 1: 15, 2: 17}[first]
        for half in (0, 1):
            for by in (-1, 1):
                block = block_at(half, first, by)
                arrived(e, half, block)
                quarter = 0 if by == -1 else 1
                put(e, half, block, quarter, 1, -by, at + quarter).start()

    def gather_rest(e):
        for half in (0, 1):
            for first in (0, -1, 1, 2):
                arrived(e, half, block_at(half, first, 2))

    def send_weight():
        return pltpu.make_async_remote_copy(
            src_ref=weight.at[core], dst_ref=weight.at[core], send_sem=w_send, recv_sem=w_recv,
            device_id=sibling, device_id_type=MESH,
        )

    def send_pair(e):
        return pltpu.make_async_remote_copy(
            src_ref=pair_out.at[e], dst_ref=pair_in.at[e], send_sem=pair_send.at[e], recv_sem=pair_recv.at[e],
            device_id=sibling, device_id_type=MESH,
        )

    def send_ring(e, way, step):
        rows = pl.ds(way * HALF, HALF) if step == 0 else pl.ds(0, HD)
        return pltpu.make_async_remote_copy(
            src_ref=ring_out.at[e, way, step, rows], dst_ref=ring_in.at[e, way, step, rows],
            send_sem=ring_send.at[e, way, step], recv_sem=ring_recv.at[e, way, step],
            device_id=up(1 - 2 * way), device_id_type=MESH,
        )

    def gradient_parts(e):
        @pl.loop(0, 2)
        def _(part):
            blocks = gath[e, pl.ds((1 - core) * DEPTH + part * 4, 4)].reshape(4 * HD, BLOCK)
            pair_out[e, pl.ds(part * 4, 4)] = (
                jnp.dot(blocks, cot[...], preferred_element_type=jnp.float32)
                .astype(jnp.bfloat16).reshape(4, HD, width)
            )
        send_pair(e).start()

        @pl.loop(0, 2)
        def _(part):
            blocks = gath[e, pl.ds(core * DEPTH + part * 4, 4)].reshape(4 * HD, BLOCK)
            kept[e, pl.ds(part * 4, 4)] = jnp.dot(
                blocks, cot[...], preferred_element_type=jnp.float32
            ).reshape(4, HD, width)

    def mix(e):
        @pl.loop(0, ROWS // 4)
        def _(part):
            blocks = gath[e, pl.ds(part * 4, 4)].reshape(4 * HD, BLOCK)
            matrix = weight[lax.div(part, 2), pl.ds(lax.rem(part, 2) * 4, 4), e].reshape(4 * HD, width)
            mixed_sum[...] += lax.dot_general(
                blocks, matrix, (((0,), (0,)), ((), ())), preferred_element_type=jnp.float32
            )

    def ring_start(e):
        send_pair(e).wait_recv()
        for way in (0, 1):
            target = shifted(z, 4, DEPTH)
            rows = pl.ds(way * HALF, HALF)
            ring_out[e, way, 0, rows] = (
                kept[e, target, rows] + pair_in[e, target, rows].astype(jnp.float32)
            ).astype(jnp.bfloat16)
            send_ring(e, way, 0).start()

    def ring_step(e, step):
        for way in (0, 1):
            send_ring(e, way, step - 1).wait_recv()
            target = shifted(z, (4 - step) * (1 - 2 * way), DEPTH)
            for half in (0, 1):
                rows = pl.ds(half * HALF, HALF)
                total = kept[e, target, rows] + pair_in[e, target, rows].astype(jnp.float32)
                if step > 1 or half == way:
                    total += ring_in[e, way, step - 1, rows].astype(jnp.float32)
                ring_out[e, way, step, rows] = total.astype(jnp.bfloat16)
            send_ring(e, way, step).start()

    def ring_end(e):
        send_ring(e, 0, 3).wait_recv()
        send_ring(e, 1, 3).wait_recv()
        total = kept[e, z] + pair_in[e, z].astype(jnp.float32)
        total += ring_in[e, 0, 3].astype(jnp.float32) + ring_in[e, 1, 3].astype(jnp.float32)
        grad_ref[e] = total.astype(jnp.bfloat16)

    kv_own(0)
    kv_own(1, (0,))
    for e in range(heads):
        queries[e] = q_ref[:, e * HD:(e + 1) * HD]
    run_max[...] = jnp.full_like(run_max, -1e30)
    run_sum[...] = jnp.zeros_like(run_sum)
    weighted[...] = jnp.zeros_like(weighted)
    mixed_sum[...] = jnp.zeros_like(mixed_sum)
    fetch_weight.wait()
    fetch_cot.wait()
    send_weight().start()

    compute(0, 0)
    kv_pass(0, 1)
    kv_own(1, (1,))
    compute(0, 1)
    kv_pass(0, 2)
    kv_own(2, (0,))
    compute(0, 2)
    kv_pass(0, 3)
    kv_pass(1, 1)
    kv_own(2, (1,))
    compute(0, 3)
    kv_pass(0, 4)
    compute(0, 4)
    gather_own(0)
    compute(1, 0)
    kv_pass(1, 2)
    kv_pass(2, 1, (0,))
    compute(1, 1)
    gather_first(0, -1)
    gather_first(0, 1)
    gather_first(0, 2)
    compute(1, 2)
    gather_line(0, 0)
    kv_pass(1, 3)
    kv_pass(2, 1, (1,))
    compute(1, 3)
    gather_line(0, -1)
    gather_line(0, 1)
    gather_line(0, 2)
    gather_rest(0)
    kv_pass(1, 4)
    compute(1, 4)
    gather_own(1)
    kv_pass(2, 2)
    gradient_parts(0)
    compute(2, 0)
    compute(2, 1)
    gather_first(1, -1)
    gather_first(1, 1)
    gather_first(1, 2)
    kv_pass(2, 3)
    compute(2, 2)
    compute(2, 3)
    ring_start(0)
    gather_line(1, 0)
    gather_line(1, -1)
    gather_line(1, 1)
    gather_line(1, 2)
    ring_step(0, 1)
    kv_pass(2, 4)
    compute(2, 4)
    gather_own(2)
    gather_rest(1)
    gradient_parts(1)
    ring_step(0, 2)
    gather_first(2, -1)
    gather_first(2, 1)
    gather_first(2, 2)
    ring_start(1)
    gather_line(2, 0)
    gather_line(2, -1)
    ring_step(0, 3)
    gather_line(2, 1)
    gather_line(2, 2)
    ring_step(1, 1)
    send_weight().wait_recv()
    gather_rest(2)
    gradient_parts(2)
    ring_step(1, 2)
    ring_start(2)
    ring_end(0)
    mix(0)
    ring_step(1, 3)
    ring_step(2, 1)
    mix(1)
    ring_step(2, 2)
    ring_end(1)
    mix(2)
    mixed_ref[...] = mixed_sum[...].astype(jnp.bfloat16)
    ring_step(2, 3)
    ring_end(2)

    send_weight().wait_send()

    @pl.loop(0, heads)
    def _(e):
        for kind in (is_key, is_value):
            for by in (1, -1):
                for hop in range(4 if (kind == is_key) == (by == 1) else 3):
                    kv(kind, e, shifted(z, -by * hop, DEPTH), by).wait_send()

            @pl.when(core == 0)
            def _():
                @pl.loop(0, DEPTH)
                def _(block):
                    hand(kind, e, block).wait_send()

        for half in (0, 1):
            @pl.loop(0, 11)
            def _(slot):
                put(e, half, me, None, 0, 1, slot).wait_send()

            @pl.loop(11, 19)
            def _(slot):
                put(e, half, me, 0, 0, 1, slot).wait_send()

        send_pair(e).wait_send()
        for way in (0, 1):
            for step in range(4):
                send_ring(e, way, step).wait_send()


def layer(block_mask, queries, keys, values, weight_half, cotangent):
    rows, width = queries.shape
    heads = width // HD
    vmem = pl.BlockSpec(memory_space=pltpu.VMEM)
    anywhere = pl.BlockSpec(memory_space=pl.ANY)
    dma = pltpu.SemaphoreType.DMA
    low, wide = jnp.bfloat16, jnp.float32
    return pl.pallas_call(
        layer_kernel,
        out_shape=(
            jax.ShapeDtypeStruct((rows, width), low),
            jax.ShapeDtypeStruct((heads, HD, width), low),
        ),
        in_specs=[pl.BlockSpec(memory_space=pltpu.SMEM), vmem, vmem, vmem, anywhere, anywhere],
        out_specs=(vmem, vmem),
        scratch_shapes=[
            pltpu.VMEM((heads, BLOCK, HD), low),
            pltpu.VMEM((2, DEPTH, heads, BLOCK, HD), low),
            pltpu.VMEM((2, DEPTH, heads, HD, BLOCK), low),
            pltpu.VMEM((heads, 1, BLOCK), wide),
            pltpu.VMEM((heads, 1, BLOCK), wide),
            pltpu.VMEM((heads, HD, BLOCK), wide),
            pltpu.VMEM((heads, ROWS, HD, BLOCK), low),
            pltpu.VMEM((2, ROWS // 2, heads, HD, width), low),
            pltpu.VMEM((BLOCK, width), low),
            pltpu.VMEM((BLOCK, width), wide),
            pltpu.VMEM((heads, DEPTH, HD, width), wide),
            pltpu.VMEM((heads, DEPTH, HD, width), low),
            pltpu.VMEM((heads, DEPTH, HD, width), low),
            pltpu.VMEM((heads, 2, 4, HD, width), low),
            pltpu.VMEM((heads, 2, 4, HD, width), low),
            dma((2, 2, DEPTH, heads)), dma((2, DEPTH, heads)), dma((2, DEPTH, heads)), dma((2, DEPTH, heads)),
            dma((heads, 2, 19)), dma((heads, 2, ROWS)), dma, dma, dma((2,)),
            dma((heads,)), dma((heads,)), dma((heads, 2, 4)), dma((heads, 2, 4)),
        ],
        compiler_params=pltpu.CompilerParams(
            collective_id=0, has_side_effects=True, vmem_limit_bytes=58 << 20
        ),
    )(block_mask, queries, keys, values, weight_half, cotangent)


def body(queries, keys, values, out_weight, cotangent, block_mask):
    width = queries.shape[1]
    mixed_out, grad_weight = layer(
        block_mask, queries, keys, values, out_weight.reshape(ROWS // 2, width // HD, HD, width), cotangent
    )
    return (mixed_out, grad_weight.reshape(width, width))


def solution(mesh):
    tokens = P(("col", "ctx"), "row")
    return jax.shard_map(
        body,
        mesh=mesh,
        in_specs=(tokens, tokens, tokens, P("col", "row"), tokens, P()),
        out_specs=(tokens, tokens),
        check_vma=False,
    )
```

```python
import functools
import math

import jax
import jax.numpy as jnp
from jax import lax
from jax.experimental import pallas as pl
from jax.experimental.pallas import tpu as pltpu
from jax.sharding import PartitionSpec as P

HD = 128
BLOCK = 512
SIDE = 4
ROWS = SIDE * SIDE
DEPTH = 8
HALF = HD // 2
QUARTER = HD // 4
MESH = pl.DeviceIdType.MESH


def shifted(value, by, size):
    return lax.rem(value + (by + size), size)


def layer_kernel(
    mask_ref, q_ref, k_ref, v_ref, w_ref, cot_ref, mixed_ref, grad_ref,
    queries, keys, values, run_max, run_sum, weighted,
    gath, weight, cot, mixed_sum, kept, pair_out, pair_in, ring_out, ring_in,
    kv_send, kv_recv, hand_send, hand_recv, ag_send, ag_recv,
    w_send, w_recv, local, pair_send, pair_recv, ring_send, ring_recv,
):
    me = lax.axis_index("row")
    core = lax.axis_index("col")
    z = lax.axis_index("ctx")
    here = (lax.rem(me, SIDE), lax.div(me, SIDE))
    heads = grad_ref.shape[0]
    width = cot_ref.shape[1]
    rate = math.log2(math.e) / math.sqrt(HD)
    stores = (keys, values)
    is_key, is_value = 0, 1
    sibling = {"col": 1 - core}

    def up(by):
        return {"ctx": shifted(z, by, DEPTH)}

    def block_at(half, first, second):
        by = (first, second) if half == 0 else (second, first)
        return shifted(here[1], by[1], SIDE) * SIDE + shifted(here[0], by[0], SIDE)

    fetch_weight = pltpu.make_async_copy(w_ref, weight.at[core], local.at[0])
    fetch_cot = pltpu.make_async_copy(cot_ref, cot, local.at[1])

    barrier = pltpu.get_barrier_semaphore()
    for first, second in ((1, 0), (-1, 0), (2, 0), (0, 1), (0, -1), (0, 2)):
        pl.semaphore_signal(barrier, inc=1, device_id={"row": block_at(0, first, second)}, device_id_type=MESH)
    for by in (1, -1):
        pl.semaphore_signal(barrier, inc=1, device_id=up(by), device_id_type=MESH)
    pl.semaphore_signal(barrier, inc=1, device_id=sibling, device_id_type=MESH)
    fetch_weight.start()
    fetch_cot.start()
    for e in range(heads):
        keys[core, z, e] = k_ref[:, e * HD:(e + 1) * HD]
    pl.semaphore_wait(barrier, 9)

    def kv(kind, e, block, by):
        ref = stores[kind].at[core, block, e]
        way = 0 if by == 1 else 1
        return pltpu.make_async_remote_copy(
            src_ref=ref, dst_ref=ref, send_sem=kv_send.at[way, kind, block, e], recv_sem=kv_recv.at[kind, block, e],
            device_id=up(by), device_id_type=MESH,
        )

    def hand(kind, e, block):
        ref = stores[kind].at[0, block, e]
        return pltpu.make_async_remote_copy(
            src_ref=ref, dst_ref=ref, send_sem=hand_send.at[kind, block, e], recv_sem=hand_recv.at[kind, block, e],
            device_id=sibling, device_id_type=MESH,
        )

    def hand_over(kind, e, block):
        pl.when(core == 0)(lambda: hand(kind, e, block).start())

    def kv_own(e, kinds=(0, 1)):
        for kind in kinds:
            if kind == is_value:
                values[core, z, e] = v_ref[:, e * HD:(e + 1) * HD].T
            kv(kind, e, z, 1).start()
            kv(kind, e, z, -1).start()
            hand_over(kind, e, z)

    def kv_pass(e, hop, kinds=(0, 1)):
        for kind in kinds:
            for by in (1, -1):
                longer = (kind == is_key) == (by == 1)
                if hop == 4 and not longer:
                    continue
                block = shifted(z, -by * hop, DEPTH)
                kv(kind, e, block, by).wait_recv()
                if hop < 3 or (hop == 3 and longer):
                    kv(kind, e, block, by).start()
                hand_over(kind, e, block)

    def absorb(e, group, blocks):
        row = core * DEPTH + z
        query = queries[e]
        parts = []
        new_max = run_max[e]
        for block in blocks:
            penalty = jnp.where(mask_ref[row, group * DEPTH + block] == 1, 0.0, 1e30)
            scores = lax.dot_general(
                keys[group, block, e], query, (((1,), (1,)), ((), ())), preferred_element_type=jnp.float32
            )
            new_max = jnp.maximum(new_max, jnp.max(scores, axis=0, keepdims=True) - penalty)
            parts.append((block, penalty, scores))
        correction = jnp.exp2((run_max[e] - new_max) * rate)
        total = run_sum[e] * correction
        product = weighted[e] * correction
        for block, penalty, scores in parts:
            probs = jnp.exp2(scores * rate - (new_max * rate + penalty))
            total += jnp.sum(probs, axis=0, keepdims=True)
            product += jnp.dot(
                values[group, block, e], probs.astype(jnp.bfloat16), preferred_element_type=jnp.float32
            )
        run_max[e] = new_max
        run_sum[e] = total
        weighted[e] = product

    def compute(e, hop):
        blocks = [shifted(z, by * hop, DEPTH) for by in ((1, -1) if 0 < hop < 4 else (1,))]

        @pl.loop(0, 1 + core)
        def _(turn):
            @pl.when(turn == 1)
            def _():
                for block in blocks:
                    for kind in (is_key, is_value):
                        hand(kind, e, block).wait_recv()
            absorb(e, core - turn, blocks)

    def put(e, half, block, quarter, leg, by, slot):
        low = half * HALF + (0 if quarter is None else quarter * QUARTER)
        ref = gath.at[e, block, pl.ds(low, HALF if quarter is None else QUARTER)]
        to = block_at(half, by, 0) if leg == 0 else block_at(half, 0, by)
        return pltpu.make_async_remote_copy(
            src_ref=ref, dst_ref=ref, send_sem=ag_send.at[e, half, slot], recv_sem=ag_recv.at[e, half, block],
            device_id={"row": to}, device_id_type=MESH,
        )

    def arrived(e, half, block):
        put(e, half, block, None, 0, 1, 0).wait_recv()

    def gather_own(e):
        gath[e, me] = (weighted[e] / run_sum[e]).astype(gath.dtype)
        for slot, (leg, by) in enumerate(((0, 1), (0, -1), (0, 2), (1, 1), (1, -1))):
            for half in (0, 1):
                put(e, half, me, None, leg, by, slot).start()

    def gather_first(e, by):
        for half in (0, 1):
            block = block_at(half, by, 0)
            arrived(e, half, block)
            base = {-1: 5, 1: 7, 2: 9}[by]
            put(e, half, block, None, 1, 1, base).start()
            put(e, half, block, None, 1, -1, base + 1).start()

    def gather_line(e, first):
        at = {0: 11, -1: 13, 1: 15, 2: 17}[first]
        for half in (0, 1):
            for by in (-1, 1):
                block = block_at(half, first, by)
                arrived(e, half, block)
                quarter = 0 if by == -1 else 1
                put(e, half, block, quarter, 1, -by, at + quarter).start()

    def gather_rest(e):
        for half in (0, 1):
            for first in (0, -1, 1, 2):
                arrived(e, half, block_at(half, first, 2))

    def send_weight():
        return pltpu.make_async_remote_copy(
            src_ref=weight.at[core], dst_ref=weight.at[core], send_sem=w_send, recv_sem=w_recv,
            device_id=sibling, device_id_type=MESH,
        )

    def send_pair(e):
        return pltpu.make_async_remote_copy(
            src_ref=pair_out.at[e], dst_ref=pair_in.at[e], send_sem=pair_send.at[e], recv_sem=pair_recv.at[e],
            device_id=sibling, device_id_type=MESH,
        )

    def send_ring(e, way, step, half):
        ref = pl.ds(half * HALF, HALF)
        return pltpu.make_async_remote_copy(
            src_ref=ring_out.at[e, way, step, ref], dst_ref=ring_in.at[e, way, step, ref],
            send_sem=ring_send.at[e, way, step, half], recv_sem=ring_recv.at[e, way, step, half],
            device_id=up(1 - 2 * way), device_id_type=MESH,
        )

    def gradient_parts(e):
        @pl.loop(0, 2)
        def _(part):
            blocks = gath[e, pl.ds((1 - core) * DEPTH + part * 4, 4)].reshape(4 * HD, BLOCK)
            pair_out[e, pl.ds(part * 4, 4)] = (
                jnp.dot(blocks, cot[...], preferred_element_type=jnp.float32)
                .astype(jnp.bfloat16).reshape(4, HD, width)
            )
        send_pair(e).start()

        @pl.loop(0, 2)
        def _(part):
            blocks = gath[e, pl.ds(core * DEPTH + part * 4, 4)].reshape(4 * HD, BLOCK)
            kept[e, pl.ds(part * 4, 4)] = jnp.dot(
                blocks, cot[...], preferred_element_type=jnp.float32
            ).reshape(4, HD, width)

    def mix(e):
        @pl.loop(0, ROWS // 4)
        def _(part):
            blocks = gath[e, pl.ds(part * 4, 4)].reshape(4 * HD, BLOCK)
            matrix = weight[lax.div(part, 2), pl.ds(lax.rem(part, 2) * 4, 4), e].reshape(4 * HD, width)
            mixed_sum[...] += lax.dot_general(
                blocks, matrix, (((0,), (0,)), ((), ())), preferred_element_type=jnp.float32
            )

    def ring_piece(e, way, step, half):
        target = shifted(z, (4 - step) * (1 - 2 * way), DEPTH)
        rows = pl.ds(half * HALF, HALF)
        total = kept[e, target, rows] + pair_in[e, target, rows].astype(jnp.float32)
        if step > (0 if half == way else 1):
            send_ring(e, way, step - 1, half).wait_recv()
            total += ring_in[e, way, step - 1, rows].astype(jnp.float32)
        ring_out[e, way, step, rows] = total.astype(jnp.bfloat16)
        send_ring(e, way, step, half).start()

    def ring_start(e):
        send_pair(e).wait_recv()
        for way in (0, 1):
            ring_piece(e, way, 0, way)
        for way in (0, 1):
            ring_piece(e, way, 1, 1 - way)

    def ring_step(e, step):
        for way in (0, 1):
            ring_piece(e, way, step, way)
        if step < 3:
            for way in (0, 1):
                ring_piece(e, way, step + 1, 1 - way)

    def ring_end(e):
        for way in (0, 1):
            for half in (0, 1):
                send_ring(e, way, 3, half).wait_recv()
        total = kept[e, z] + pair_in[e, z].astype(jnp.float32)
        total += ring_in[e, 0, 3].astype(jnp.float32) + ring_in[e, 1, 3].astype(jnp.float32)
        grad_ref[e] = total.astype(jnp.bfloat16)

    kv_own(0)
    kv_own(1, (0,))
    for e in range(heads):
        queries[e] = q_ref[:, e * HD:(e + 1) * HD]
    run_max[...] = jnp.full_like(run_max, -1e30)
    run_sum[...] = jnp.zeros_like(run_sum)
    weighted[...] = jnp.zeros_like(weighted)
    mixed_sum[...] = jnp.zeros_like(mixed_sum)
    fetch_weight.wait()
    fetch_cot.wait()
    send_weight().start()

    compute(0, 0)
    kv_pass(0, 1)
    kv_own(1, (1,))
    compute(0, 1)
    kv_pass(0, 2)
    kv_own(2, (0,))
    compute(0, 2)
    kv_pass(0, 3)
    kv_pass(1, 1)
    kv_own(2, (1,))
    compute(0, 3)
    kv_pass(0, 4)
    compute(0, 4)
    gather_own(0)
    compute(1, 0)
    kv_pass(1, 2)
    kv_pass(2, 1, (0,))
    compute(1, 1)
    gather_first(0, -1)
    gather_first(0, 1)
    gather_first(0, 2)
    compute(1, 2)
    kv_pass(1, 3)
    kv_pass(2, 1, (1,))
    gather_line(0, 0)
    gather_line(0, -1)
    compute(1, 3)
    gather_line(0, 1)
    gather_line(0, 2)
    kv_pass(1, 4)
    compute(1, 4)
    gather_own(1)
    kv_pass(2, 2)
    gather_rest(0)
    gradient_parts(0)
    compute(2, 0)
    compute(2, 1)
    kv_pass(2, 3)
    ring_start(0)
    gather_first(1, -1)
    gather_first(1, 1)
    gather_first(1, 2)
    compute(2, 2)
    compute(2, 3)
    gather_line(1, 0)
    gather_line(1, -1)
    gather_line(1, 1)
    gather_line(1, 2)
    ring_step(0, 1)
    kv_pass(2, 4)
    compute(2, 4)
    gather_own(2)
    gather_rest(1)
    gradient_parts(1)
    ring_step(0, 2)
    gather_first(2, -1)
    gather_first(2, 1)
    gather_first(2, 2)
    ring_start(1)
    gather_line(2, 0)
    gather_line(2, -1)
    ring_step(0, 3)
    gather_line(2, 1)
    gather_line(2, 2)
    ring_step(1, 1)
    send_weight().wait_recv()
    gather_rest(2)
    gradient_parts(2)
    ring_step(1, 2)
    ring_start(2)
    ring_end(0)
    mix(0)
    ring_step(1, 3)
    ring_step(2, 1)
    mix(1)
    ring_step(2, 2)
    ring_end(1)
    mix(2)
    mixed_ref[...] = mixed_sum[...].astype(jnp.bfloat16)
    ring_step(2, 3)
    ring_end(2)

    send_weight().wait_send()

    @pl.loop(0, heads)
    def _(e):
        for kind in (is_key, is_value):
            for by in (1, -1):
                for hop in range(4 if (kind == is_key) == (by == 1) else 3):
                    kv(kind, e, shifted(z, -by * hop, DEPTH), by).wait_send()

            @pl.when(core == 0)
            def _():
                @pl.loop(0, DEPTH)
                def _(block):
                    hand(kind, e, block).wait_send()

        for half in (0, 1):
            @pl.loop(0, 11)
            def _(slot):
                put(e, half, me, None, 0, 1, slot).wait_send()

            @pl.loop(11, 19)
            def _(slot):
                put(e, half, me, 0, 0, 1, slot).wait_send()

        send_pair(e).wait_send()
        for way in (0, 1):
            for half in (0, 1):
                for step in range(0 if half == way else 1, 4):
                    send_ring(e, way, step, half).wait_send()


def layer(block_mask, queries, keys, values, weight_half, cotangent):
    rows, width = queries.shape
    heads = width // HD
    vmem = pl.BlockSpec(memory_space=pltpu.VMEM)
    anywhere = pl.BlockSpec(memory_space=pl.ANY)
    dma = pltpu.SemaphoreType.DMA
    low, wide = jnp.bfloat16, jnp.float32
    return pl.pallas_call(
        layer_kernel,
        out_shape=(
            jax.ShapeDtypeStruct((rows, width), low),
            jax.ShapeDtypeStruct((heads, HD, width), low),
        ),
        in_specs=[pl.BlockSpec(memory_space=pltpu.SMEM), vmem, vmem, vmem, anywhere, anywhere],
        out_specs=(vmem, vmem),
        scratch_shapes=[
            pltpu.VMEM((heads, BLOCK, HD), low),
            pltpu.VMEM((2, DEPTH, heads, BLOCK, HD), low),
            pltpu.VMEM((2, DEPTH, heads, HD, BLOCK), low),
            pltpu.VMEM((heads, 1, BLOCK), wide),
            pltpu.VMEM((heads, 1, BLOCK), wide),
            pltpu.VMEM((heads, HD, BLOCK), wide),
            pltpu.VMEM((heads, ROWS, HD, BLOCK), low),
            pltpu.VMEM((2, ROWS // 2, heads, HD, width), low),
            pltpu.VMEM((BLOCK, width), low),
            pltpu.VMEM((BLOCK, width), wide),
            pltpu.VMEM((heads, DEPTH, HD, width), wide),
            pltpu.VMEM((heads, DEPTH, HD, width), low),
            pltpu.VMEM((heads, DEPTH, HD, width), low),
            pltpu.VMEM((heads, 2, 4, HD, width), low),
            pltpu.VMEM((heads, 2, 4, HD, width), low),
            dma((2, 2, DEPTH, heads)), dma((2, DEPTH, heads)), dma((2, DEPTH, heads)), dma((2, DEPTH, heads)),
            dma((heads, 2, 19)), dma((heads, 2, ROWS)), dma, dma, dma((2,)),
            dma((heads,)), dma((heads,)), dma((heads, 2, 4, 2)), dma((heads, 2, 4, 2)),
        ],
        compiler_params=pltpu.CompilerParams(
            collective_id=0, has_side_effects=True, vmem_limit_bytes=58 << 20
        ),
    )(block_mask, queries, keys, values, weight_half, cotangent)


def body(queries, keys, values, out_weight, cotangent, block_mask):
    width = queries.shape[1]
    mixed_out, grad_weight = layer(
        block_mask, queries, keys, values, out_weight.reshape(ROWS // 2, width // HD, HD, width), cotangent
    )
    return (mixed_out, grad_weight.reshape(width, width))


def solution(mesh):
    tokens = P(("col", "ctx"), "row")
    return jax.shard_map(
        body,
        mesh=mesh,
        in_specs=(tokens, tokens, tokens, P("col", "row"), tokens, P()),
        out_specs=(tokens, tokens),
        check_vma=False,
    )
```

```python
import functools
import math

import jax
import jax.numpy as jnp
from jax import lax
from jax.experimental import pallas as pl
from jax.experimental.pallas import tpu as pltpu
from jax.sharding import PartitionSpec as P

HD = 128
BLOCK = 512
SIDE = 4
ROWS = SIDE * SIDE
DEPTH = 8
HALF = HD // 2
QUARTER = HD // 4
MESH = pl.DeviceIdType.MESH


def shifted(value, by, size):
    return lax.rem(value + (by + size), size)


def layer_kernel(
    mask_ref, q_ref, k_ref, v_ref, w_ref, cot_ref, mixed_ref, grad_ref,
    queries, keys, values, run_max, run_sum, weighted,
    gath, weight, cot, mixed_sum, kept, pair_out, pair_in, ring_out, ring_in,
    kv_send, kv_recv, hand_send, hand_recv, ag_send, ag_recv,
    w_send, w_recv, local, pair_send, pair_recv, ring_send, ring_recv,
):
    me = lax.axis_index("row")
    core = lax.axis_index("col")
    z = lax.axis_index("ctx")
    here = (lax.rem(me, SIDE), lax.div(me, SIDE))
    heads = grad_ref.shape[0]
    width = cot_ref.shape[1]
    rate = math.log2(math.e) / math.sqrt(HD)
    stores = (keys, values)
    is_key, is_value = 0, 1
    sibling = {"col": 1 - core}

    def up(by):
        return {"ctx": shifted(z, by, DEPTH)}

    def block_at(half, first, second):
        by = (first, second) if half == 0 else (second, first)
        return shifted(here[1], by[1], SIDE) * SIDE + shifted(here[0], by[0], SIDE)

    fetch_weight = pltpu.make_async_copy(w_ref, weight.at[core], local.at[0])
    fetch_cot = pltpu.make_async_copy(cot_ref, cot, local.at[1])

    barrier = pltpu.get_barrier_semaphore()
    for first, second in ((1, 0), (-1, 0), (2, 0), (0, 1), (0, -1), (0, 2)):
        pl.semaphore_signal(barrier, inc=1, device_id={"row": block_at(0, first, second)}, device_id_type=MESH)
    for by in (1, -1):
        pl.semaphore_signal(barrier, inc=1, device_id=up(by), device_id_type=MESH)
    pl.semaphore_signal(barrier, inc=1, device_id=sibling, device_id_type=MESH)
    fetch_weight.start()
    fetch_cot.start()
    for e in range(heads):
        keys[core, z, e] = k_ref[:, e * HD:(e + 1) * HD]
    pl.semaphore_wait(barrier, 9)

    def kv(kind, e, block, by):
        ref = stores[kind].at[core, block, e]
        way = 0 if by == 1 else 1
        return pltpu.make_async_remote_copy(
            src_ref=ref, dst_ref=ref, send_sem=kv_send.at[way, kind, block, e], recv_sem=kv_recv.at[kind, block, e],
            device_id=up(by), device_id_type=MESH,
        )

    def hand(kind, e, block):
        ref = stores[kind].at[0, block, e]
        return pltpu.make_async_remote_copy(
            src_ref=ref, dst_ref=ref, send_sem=hand_send.at[kind, block, e], recv_sem=hand_recv.at[kind, block, e],
            device_id=sibling, device_id_type=MESH,
        )

    def hand_over(kind, e, block):
        pl.when(core == 0)(lambda: hand(kind, e, block).start())

    def kv_own(e, kinds=(0, 1)):
        for kind in kinds:
            if kind == is_value:
                values[core, z, e] = v_ref[:, e * HD:(e + 1) * HD].T
            kv(kind, e, z, 1).start()
            kv(kind, e, z, -1).start()
            hand_over(kind, e, z)

    def kv_pass(e, hop, kinds=(0, 1)):
        for kind in kinds:
            for by in (1, -1):
                longer = (kind == is_key) == (by == 1)
                if hop == 4 and not longer:
                    continue
                block = shifted(z, -by * hop, DEPTH)
                kv(kind, e, block, by).wait_recv()
                if hop < 3 or (hop == 3 and longer):
                    kv(kind, e, block, by).start()
                hand_over(kind, e, block)

    def absorb(e, group, blocks):
        row = core * DEPTH + z
        query = queries[e]
        parts = []
        new_max = run_max[e]
        for block in blocks:
            penalty = jnp.where(mask_ref[row, group * DEPTH + block] == 1, 0.0, 1e30)
            scores = lax.dot_general(
                keys[group, block, e], query, (((1,), (1,)), ((), ())), preferred_element_type=jnp.float32
            )
            new_max = jnp.maximum(new_max, jnp.max(scores, axis=0, keepdims=True) - penalty)
            parts.append((block, penalty, scores))
        correction = jnp.exp2((run_max[e] - new_max) * rate)
        total = run_sum[e] * correction
        product = weighted[e] * correction
        for block, penalty, scores in parts:
            probs = jnp.exp2(scores * rate - (new_max * rate + penalty))
            total += jnp.sum(probs, axis=0, keepdims=True)
            product += jnp.dot(
                values[group, block, e], probs.astype(jnp.bfloat16), preferred_element_type=jnp.float32
            )
        run_max[e] = new_max
        run_sum[e] = total
        weighted[e] = product

    def compute(e, hop):
        blocks = [shifted(z, by * hop, DEPTH) for by in ((1, -1) if 0 < hop < 4 else (1,))]

        @pl.loop(0, 1 + core)
        def _(turn):
            @pl.when(turn == 1)
            def _():
                for block in blocks:
                    for kind in (is_key, is_value):
                        hand(kind, e, block).wait_recv()
            absorb(e, core - turn, blocks)

    def put(e, half, block, quarter, leg, by, slot):
        low = half * HALF + (0 if quarter is None else quarter * QUARTER)
        ref = gath.at[e, block, pl.ds(low, HALF if quarter is None else QUARTER)]
        to = block_at(half, by, 0) if leg == 0 else block_at(half, 0, by)
        return pltpu.make_async_remote_copy(
            src_ref=ref, dst_ref=ref, send_sem=ag_send.at[e, half, slot], recv_sem=ag_recv.at[e, half, block],
            device_id={"row": to}, device_id_type=MESH,
        )

    def arrived(e, half, block):
        put(e, half, block, None, 0, 1, 0).wait_recv()

    def gather_own(e):
        gath[e, me] = (weighted[e] / run_sum[e]).astype(gath.dtype)
        for slot, (leg, by) in enumerate(((0, 1), (0, -1), (0, 2), (1, 1), (1, -1))):
            for half in (0, 1):
                put(e, half, me, None, leg, by, slot).start()

    def gather_first(e, by):
        for half in (0, 1):
            block = block_at(half, by, 0)
            arrived(e, half, block)
            base = {-1: 5, 1: 7, 2: 9}[by]
            put(e, half, block, None, 1, 1, base).start()
            put(e, half, block, None, 1, -1, base + 1).start()

    def gather_line(e, first):
        at = {0: 11, -1: 13, 1: 15, 2: 17}[first]
        for half in (0, 1):
            for by in (-1, 1):
                block = block_at(half, first, by)
                arrived(e, half, block)
                quarter = 0 if by == -1 else 1
                put(e, half, block, quarter, 1, -by, at + quarter).start()

    def gather_rest(e):
        for half in (0, 1):
            for first in (0, -1, 1, 2):
                arrived(e, half, block_at(half, first, 2))

    def send_weight():
        return pltpu.make_async_remote_copy(
            src_ref=weight.at[core], dst_ref=weight.at[core], send_sem=w_send, recv_sem=w_recv,
            device_id=sibling, device_id_type=MESH,
        )

    def send_pair(e):
        return pltpu.make_async_remote_copy(
            src_ref=pair_out.at[e], dst_ref=pair_in.at[e], send_sem=pair_send.at[e], recv_sem=pair_recv.at[e],
            device_id=sibling, device_id_type=MESH,
        )

    def send_ring(e, way, step, half):
        ref = pl.ds(half * HALF, HALF)
        return pltpu.make_async_remote_copy(
            src_ref=ring_out.at[e, way, step, ref], dst_ref=ring_in.at[e, way, step, ref],
            send_sem=ring_send.at[e, way, step, half], recv_sem=ring_recv.at[e, way, step, half],
            device_id=up(1 - 2 * way), device_id_type=MESH,
        )

    def gradient_parts(e):
        @pl.loop(0, 2)
        def _(part):
            blocks = gath[e, pl.ds((1 - core) * DEPTH + part * 4, 4)].reshape(4 * HD, BLOCK)
            pair_out[e, pl.ds(part * 4, 4)] = (
                jnp.dot(blocks, cot[...], preferred_element_type=jnp.float32)
                .astype(jnp.bfloat16).reshape(4, HD, width)
            )
        send_pair(e).start()

        @pl.loop(0, 2)
        def _(part):
            blocks = gath[e, pl.ds(core * DEPTH + part * 4, 4)].reshape(4 * HD, BLOCK)
            kept[e, pl.ds(part * 4, 4)] = jnp.dot(
                blocks, cot[...], preferred_element_type=jnp.float32
            ).reshape(4, HD, width)

    def mix(e):
        @pl.loop(0, ROWS // 4)
        def _(part):
            blocks = gath[e, pl.ds(part * 4, 4)].reshape(4 * HD, BLOCK)
            matrix = weight[lax.div(part, 2), pl.ds(lax.rem(part, 2) * 4, 4), e].reshape(4 * HD, width)
            mixed_sum[...] += lax.dot_general(
                blocks, matrix, (((0,), (0,)), ((), ())), preferred_element_type=jnp.float32
            )

    def ring_piece(e, way, step, half):
        target = shifted(z, (4 - step) * (1 - 2 * way), DEPTH)
        rows = pl.ds(half * HALF, HALF)
        total = kept[e, target, rows] + pair_in[e, target, rows].astype(jnp.float32)
        if step > (0 if half == way else 1):
            send_ring(e, way, step - 1, half).wait_recv()
            total += ring_in[e, way, step - 1, rows].astype(jnp.float32)
        ring_out[e, way, step, rows] = total.astype(jnp.bfloat16)
        send_ring(e, way, step, half).start()

    def ring_start(e):
        send_pair(e).wait_recv()
        for way in (0, 1):
            ring_piece(e, way, 0, way)
        for way in (0, 1):
            ring_piece(e, way, 1, 1 - way)

    def ring_step(e, step):
        for way in (0, 1):
            ring_piece(e, way, step, way)
        if step < 3:
            for way in (0, 1):
                ring_piece(e, way, step + 1, 1 - way)

    def ring_end(e):
        for way in (0, 1):
            for half in (0, 1):
                send_ring(e, way, 3, half).wait_recv()
        total = kept[e, z] + pair_in[e, z].astype(jnp.float32)
        total += ring_in[e, 0, 3].astype(jnp.float32) + ring_in[e, 1, 3].astype(jnp.float32)
        grad_ref[e] = total.astype(jnp.bfloat16)

    def drain_kv():
        send_weight().wait_send()

        @pl.loop(0, heads)
        def _(e):
            for kind in (is_key, is_value):
                for by in (1, -1):
                    for hop in range(4 if (kind == is_key) == (by == 1) else 3):
                        kv(kind, e, shifted(z, -by * hop, DEPTH), by).wait_send()

                @pl.when(core == 0)
                def _():
                    @pl.loop(0, DEPTH)
                    def _(block):
                        hand(kind, e, block).wait_send()

    def drain_gather():
        @pl.loop(0, heads)
        def _(e):
            send_pair(e).wait_send()
            for half in (0, 1):
                @pl.loop(0, 11)
                def _(slot):
                    put(e, half, me, None, 0, 1, slot).wait_send()

                @pl.loop(11, 19)
                def _(slot):
                    put(e, half, me, 0, 0, 1, slot).wait_send()

    def drain_ring(e, steps):
        for way in (0, 1):
            for half in (0, 1):
                for step in steps:
                    if step > 0 or half == way:
                        send_ring(e, way, step, half).wait_send()

    kv_own(0)
    kv_own(1, (0,))
    for e in range(heads):
        queries[e] = q_ref[:, e * HD:(e + 1) * HD]
    run_max[...] = jnp.full_like(run_max, -1e30)
    run_sum[...] = jnp.zeros_like(run_sum)
    weighted[...] = jnp.zeros_like(weighted)
    mixed_sum[...] = jnp.zeros_like(mixed_sum)
    fetch_weight.wait()
    fetch_cot.wait()
    send_weight().start()

    compute(0, 0)
    kv_pass(0, 1)
    kv_own(1, (1,))
    compute(0, 1)
    kv_pass(0, 2)
    kv_own(2, (0,))
    compute(0, 2)
    kv_pass(0, 3)
    kv_pass(1, 1)
    kv_own(2, (1,))
    compute(0, 3)
    kv_pass(0, 4)
    compute(0, 4)
    gather_own(0)
    compute(1, 0)
    kv_pass(1, 2)
    kv_pass(2, 1, (0,))
    compute(1, 1)
    gather_first(0, -1)
    gather_first(0, 1)
    gather_first(0, 2)
    compute(1, 2)
    kv_pass(1, 3)
    kv_pass(2, 1, (1,))
    gather_line(0, 0)
    gather_line(0, -1)
    compute(1, 3)
    gather_line(0, 1)
    gather_line(0, 2)
    kv_pass(1, 4)
    compute(1, 4)
    gather_own(1)
    kv_pass(2, 2)
    gather_rest(0)
    gradient_parts(0)
    compute(2, 0)
    compute(2, 1)
    kv_pass(2, 3)
    ring_start(0)
    gather_first(1, -1)
    gather_first(1, 1)
    gather_first(1, 2)
    compute(2, 2)
    compute(2, 3)
    gather_line(1, 0)
    gather_line(1, -1)
    gather_line(1, 1)
    gather_line(1, 2)
    ring_step(0, 1)
    kv_pass(2, 4)
    compute(2, 4)
    gather_own(2)
    gather_rest(1)
    gradient_parts(1)
    ring_step(0, 2)
    gather_first(2, -1)
    gather_first(2, 1)
    gather_first(2, 2)
    ring_start(1)
    gather_line(2, 0)
    gather_line(2, -1)
    ring_step(0, 3)
    gather_line(2, 1)
    gather_line(2, 2)
    ring_step(1, 1)
    send_weight().wait_recv()
    gather_rest(2)
    gradient_parts(2)
    ring_step(1, 2)
    ring_start(2)
    ring_end(0)
    mix(0)
    ring_step(1, 3)
    ring_step(2, 1)
    mix(1)
    drain_kv()
    ring_step(2, 2)
    ring_end(1)
    mix(2)
    drain_gather()
    mixed_ref[...] = mixed_sum[...].astype(jnp.bfloat16)
    ring_step(2, 3)
    drain_ring(0, range(4))
    drain_ring(1, range(4))
    drain_ring(2, range(3))
    ring_end(2)
    drain_ring(2, (3,))


def layer(block_mask, queries, keys, values, weight_half, cotangent):
    rows, width = queries.shape
    heads = width // HD
    vmem = pl.BlockSpec(memory_space=pltpu.VMEM)
    anywhere = pl.BlockSpec(memory_space=pl.ANY)
    dma = pltpu.SemaphoreType.DMA
    low, wide = jnp.bfloat16, jnp.float32
    return pl.pallas_call(
        layer_kernel,
        out_shape=(
            jax.ShapeDtypeStruct((rows, width), low),
            jax.ShapeDtypeStruct((heads, HD, width), low),
        ),
        in_specs=[pl.BlockSpec(memory_space=pltpu.SMEM), vmem, vmem, vmem, anywhere, anywhere],
        out_specs=(vmem, vmem),
        scratch_shapes=[
            pltpu.VMEM((heads, BLOCK, HD), low),
            pltpu.VMEM((2, DEPTH, heads, BLOCK, HD), low),
            pltpu.VMEM((2, DEPTH, heads, HD, BLOCK), low),
            pltpu.VMEM((heads, 1, BLOCK), wide),
            pltpu.VMEM((heads, 1, BLOCK), wide),
            pltpu.VMEM((heads, HD, BLOCK), wide),
            pltpu.VMEM((heads, ROWS, HD, BLOCK), low),
            pltpu.VMEM((2, ROWS // 2, heads, HD, width), low),
            pltpu.VMEM((BLOCK, width), low),
            pltpu.VMEM((BLOCK, width), wide),
            pltpu.VMEM((heads, DEPTH, HD, width), wide),
            pltpu.VMEM((heads, DEPTH, HD, width), low),
            pltpu.VMEM((heads, DEPTH, HD, width), low),
            pltpu.VMEM((heads, 2, 4, HD, width), low),
            pltpu.VMEM((heads, 2, 4, HD, width), low),
            dma((2, 2, DEPTH, heads)), dma((2, DEPTH, heads)), dma((2, DEPTH, heads)), dma((2, DEPTH, heads)),
            dma((heads, 2, 19)), dma((heads, 2, ROWS)), dma, dma, dma((2,)),
            dma((heads,)), dma((heads,)), dma((heads, 2, 4, 2)), dma((heads, 2, 4, 2)),
        ],
        compiler_params=pltpu.CompilerParams(
            collective_id=0, has_side_effects=True, vmem_limit_bytes=58 << 20
        ),
    )(block_mask, queries, keys, values, weight_half, cotangent)


def body(queries, keys, values, out_weight, cotangent, block_mask):
    width = queries.shape[1]
    mixed_out, grad_weight = layer(
        block_mask, queries, keys, values, out_weight.reshape(ROWS // 2, width // HD, HD, width), cotangent
    )
    return (mixed_out, grad_weight.reshape(width, width))


def solution(mesh):
    tokens = P(("col", "ctx"), "row")
    return jax.shard_map(
        body,
        mesh=mesh,
        in_specs=(tokens, tokens, tokens, P("col", "row"), tokens, P()),
        out_specs=(tokens, tokens),
        check_vma=False,
    )
```
